32 devices in a mesh: group: 8 (over z, core), tensor: 4 (over y, x).
Axes of the slice: x: 2, y: 2, z: 4, core: 2. Of those that a mesh axis runs over, the one named last changes fastest.
Arguments:
- queries: bfloat16 [96, 4, 8192], P('group', None, 'tensor'), may hold values from -603 to 603
- new_entries: bfloat16 [96, 4, 2048], P('group'), may hold values from -6 to 6
- resident_cache: bfloat16 [32, 512, 2048], P('group', 'tensor'), may hold values from -6 to 6
- prefill_cache: bfloat16 [64, 512, 2048], P('group', 'tensor'), may hold values from -6 to 6
- resident_kept: int32 [32], replicated, may hold values from 256 to 512, as said below
- kept_tokens: int32 [64], replicated, may hold values from 1 to 512, as said below
- prefill_slot: int32 [64], replicated, may hold values from 0 to 63, as said below
- decode_slot: int32 [64], replicated, may hold values from 4 to 95, as said below
Outputs:
- attended: bfloat16 [96, 4, 8192], P('group', None, 'tensor')
The draws below stay inside these ranges and needn't reach their ends.
Inputs may be any that keep to these rules, and one draw needn't show every extreme that they name: `kept_tokens`: some request keeps exactly 512 positions. `prefill_slot`: A permutation of the 64 prefill slots; slot s lies in prefill group s // 8. `decode_slot`: every slot g * 12 + l with l >= 4 is named by exactly one request; from one prefill group to one decode group go at most 1 request, and exactly 1 for some pairs. `resident_kept`: some resident request keeps exactly 512 positions.
All inputs are finite; a program needn't handle non-finite values.
Results may differ from the reference program's by a relative error of at most 0.0044.
Values may be sent and summed in bfloat16 or wider, within the bound.
A program may use at most 128 MiB of HBM per device.

```python
import math
import jax
import jax.numpy as jnp
from jax import lax

H = 64
KVH = 8
HD = 128
STEPS = 4
CAP = 512
MIG_DEV = 8
RES_DEV = 4
DSLOTS = 96
REQS = 64
PAIR_MOST = 1
N_GROUP = 8


def migration_plan(key):
    base = jax.random.fold_in(key, 7)
    subkeys = jax.random.split(base, 5)
    slot_count = MIG_DEV * N_GROUP
    rotation = jax.random.randint(subkeys[0], (), 0, 4)
    every_slot = jnp.arange(slot_count, dtype=jnp.int32)
    home_group = every_slot // MIG_DEV
    home_local = every_slot % MIG_DEV
    load_level = 1 + (home_group + rotation) % 4
    jitter = jax.random.randint(subkeys[1], (slot_count,), 0, CAP // 8)
    jitter = jnp.where((load_level == 4) & (home_local == 0), 0, jitter)
    kept_by_slot = load_level * (CAP // 4) - jitter
    group_order = jax.random.permutation(subkeys[2], N_GROUP).astype(jnp.int32)
    local_order = jax.random.permutation(subkeys[3], MIG_DEV).astype(jnp.int32)
    lane_index = home_local // PAIR_MOST
    target_group = group_order[(home_group + lane_index) % N_GROUP]
    target_local = RES_DEV + local_order[lane_index * PAIR_MOST + home_local % PAIR_MOST]
    target_slot = target_group * (RES_DEV + MIG_DEV) + target_local
    request_slot = jax.random.permutation(subkeys[4], slot_count).astype(jnp.int32)
    return (kept_by_slot[request_slot], request_slot, target_slot[request_slot])


def draw_kept_tokens(key, part):
    return migration_plan(key)[0].astype(jnp.int32)


def draw_prefill_slot(key, part):
    return migration_plan(key)[1].astype(jnp.int32)


def draw_decode_slot(key, part):
    return migration_plan(key)[2].astype(jnp.int32)


def draw_resident_kept(key, part):
    sub_key = jax.random.fold_in(key, 11)
    picked = jax.random.randint(sub_key, (N_GROUP * RES_DEV,), CAP // 2, CAP + 1)
    return jnp.where(jnp.arange(N_GROUP * RES_DEV) == 0, CAP, picked).astype(jnp.int32)


def token_draws(key):
    base = jax.random.fold_in(key, 23)
    subkeys = jax.random.split(base, 2)
    row_total = DSLOTS
    new_part = jnp.clip(jax.random.normal(subkeys[0], (row_total, STEPS, 2, KVH, HD), jnp.float32), -6.0, 6.0)
    spread_part = jnp.clip(jax.random.normal(subkeys[1], (row_total, STEPS, KVH, H // KVH, HD), jnp.float32), -6.0, 6.0)
    asking = spread_part + 0.5 * new_part[:, :, 0, :, None, :]
    return (asking.reshape(row_total, STEPS, H * HD), new_part.reshape(row_total, STEPS, 2 * KVH * HD))


def draw_queries(key, part):
    return token_draws(key)[0].astype(jnp.bfloat16)


def draw_new_entries(key, part):
    return token_draws(key)[1].astype(jnp.bfloat16)


def level_of(own_key, dims, cuts, smallest, largest):
    level = 1.0
    for position, parts in cuts:
        heights = jax.random.uniform(jax.random.fold_in(jax.random.fold_in(own_key, 6), position), (parts,), jnp.float32, smallest / len(cuts), largest / len(cuts))
        level = level * jnp.repeat(jnp.exp(heights), dims[position] // parts).reshape((-1,) + (1,) * (len(dims) - 1 - position))
    return level


def centred(own_key, shape, spread, reach, shards=(), kind=jnp.bfloat16):
    factor_of = level_of(own_key, shape, shards, -0.22, 0.18) if shards else 1.0
    result = jax.random.normal(own_key, shape, jnp.float32) * spread * factor_of
    return jnp.minimum(jnp.maximum(result, -reach), reach).astype(kind)


def setup_inputs(seed: int = 0) -> dict:
    splits = jax.random.split(jax.random.key(seed), 9)
    return {
        "queries": draw_queries(jax.random.fold_in(splits[8], 71), 0),
        "new_entries": draw_new_entries(jax.random.fold_in(splits[8], 71), 0),
        "resident_cache": centred(splits[2], (N_GROUP * RES_DEV, CAP, 2 * KVH * HD), 1.0, 6.0, ((0, 8), (1, 4))),
        "prefill_cache": centred(splits[3], (REQS, CAP, 2 * KVH * HD), 1.0, 6.0, ((0, 8), (1, 4))),
        "resident_kept": draw_resident_kept(jax.random.fold_in(splits[8], 71), 0),
        "kept_tokens": draw_kept_tokens(jax.random.fold_in(splits[8], 71), 0),
        "prefill_slot": draw_prefill_slot(jax.random.fold_in(splits[8], 71), 0),
        "decode_slot": draw_decode_slot(jax.random.fold_in(splits[8], 71), 0),
    }


def attend_one(asking, newest_in, stored, length):
    sharing = H // KVH
    temper = 1.0 / math.sqrt(HD)
    asked_rows = asking.astype(jnp.float32).reshape(STEPS, KVH, sharing, HD)
    entries = stored.astype(jnp.float32).reshape(CAP, 2, KVH, HD)
    newest = newest_in.astype(jnp.float32).reshape(STEPS, 2, KVH, HD)
    old_scores = jnp.einsum('tkgd,pkd->tkgp', asked_rows, entries[:, 0]) * temper
    new_scores = jnp.einsum('tkgd,ukd->tkgu', asked_rows, newest[:, 0]) * temper
    old_usable = (jnp.arange(CAP) < length)[None, None, None, :]
    new_usable = (jnp.arange(STEPS)[None, :] <= jnp.arange(STEPS)[:, None])[:, None, None, :]
    highest = jnp.maximum(lax.optimization_barrier(jnp.max(jnp.where(old_usable, old_scores, -1e+30), axis=3)), lax.optimization_barrier(jnp.max(jnp.where(new_usable, new_scores, -1e+30), axis=3)))
    old_weights = jnp.where(old_usable, jnp.exp(old_scores - highest[..., None]), 0.0)
    new_weights = jnp.where(new_usable, jnp.exp(new_scores - highest[..., None]), 0.0)
    totals = lax.optimization_barrier(jnp.sum(old_weights, axis=3)) + lax.optimization_barrier(jnp.sum(new_weights, axis=3))
    old_rounded = lax.optimization_barrier(old_weights.astype(jnp.bfloat16)).astype(jnp.float32)
    new_rounded = lax.optimization_barrier(new_weights.astype(jnp.bfloat16)).astype(jnp.float32)
    blended = jnp.einsum('tkgp,pkd->tkgd', old_rounded, entries[:, 1]) + jnp.einsum('tkgu,ukd->tkgd', new_rounded, newest[:, 1])
    return (blended / totals[..., None]).reshape(STEPS, H * HD).astype(jnp.bfloat16)

def reference(queries, new_entries, resident_cache, prefill_cache, resident_kept, kept_tokens, prefill_slot, decode_slot):
    per_group = RES_DEV + MIG_DEV
    total_slots = N_GROUP * per_group
    source = jnp.zeros((total_slots,), jnp.int32).at[decode_slot].set(prefill_slot.astype(jnp.int32))
    moved_len = jnp.zeros((total_slots,), jnp.int32).at[decode_slot].set(kept_tokens.astype(jnp.int32))
    everyone = jnp.arange(total_slots, dtype=jnp.int32)
    owner_group = everyone // per_group
    within = everyone % per_group
    is_resident = within < RES_DEV
    resident_row = (owner_group * RES_DEV + jnp.minimum(within, RES_DEV - 1)).astype(jnp.int32)
    lengths = jnp.where(is_resident, resident_kept[resident_row], moved_len)

    def handle(record):
        slot_id, resident_id, source_id, is_local, length = record
        stored = jnp.where(is_local, resident_cache[resident_id], prefill_cache[source_id])
        return attend_one(queries[slot_id], new_entries[slot_id], stored, length)
    return lax.map(handle, (everyone, resident_row, source, is_resident, lengths))
```

```python
import functools
import math

import jax
import jax.numpy as jnp
from jax import lax
from jax.experimental import pallas as pl
from jax.experimental.pallas import tpu as pltpu
from jax.sharding import PartitionSpec as P

H = 64
KVH = 8
HD = 128
STEPS = 4
MIG_DEV = 8
RES_DEV = 4
PER_GROUP = RES_DEV + MIG_DEV
BATCH = 4

NEG_FLOOR = -1e30
SCALE = 1.0 / math.sqrt(HD)
MESH = pl.DeviceIdType.MESH
F32 = jnp.float32
BF16 = jnp.bfloat16
NT = (((1,), (1,)), ((), ()))
TN = (((0,), (0,)), ((), ()))


def flipped(v, mask):
    out, bit = v, 1
    while bit <= mask:
        if mask & bit:
            out = out + bit * (1 - 2 * lax.rem(lax.div(v, bit), 2))
        bit *= 2
    return out


def fill_table(peers, sources, g, kept_v, home_v, dest_v, tab_v):
    G = len(peers)
    shape = (2 * G, dest_v.shape[1])
    n = lax.broadcasted_iota(jnp.int32, shape, 0)
    dest = jnp.broadcast_to(dest_v[...], shape)
    home = jnp.broadcast_to(home_v[...], shape)
    kept = jnp.broadcast_to(kept_v[...], shape)
    dest_group, home_group = lax.div(dest, PER_GROUP), lax.div(home, MIG_DEV)
    other = jnp.zeros(shape, jnp.int32)
    for k in range(G):
        other = jnp.where(n == k, peers[k], other)
        other = jnp.where(n == G + k, sources[k], other)
    arriving = (n < G) & (dest_group == g) & (home_group == other)
    leaving = (n >= G) & (home_group == g) & (dest_group == other)
    picked = jnp.where(arriving, dest - dest_group * PER_GROUP, 0)
    held = home - home_group * MIG_DEV + MIG_DEV * kept
    picked = picked + jnp.where(leaving, held, 0)
    total = jnp.sum(picked, axis=1, keepdims=True)
    tab_v[...] = jnp.broadcast_to(total, tab_v.shape)


def kernel(
    G,
    T,
    kept_hbm,
    home_hbm,
    dest_hbm,
    stay_hbm,
    q_hbm,
    new_hbm,
    res_hbm,
    pre_hbm,
    out,
    kept_v,
    home_v,
    dest_v,
    kept,
    tab_v,
    tab_s,
    q_in,
    new_in,
    res,
    pre,
    qall,
    zq,
    stage,
    obuf,
    rbuf,
    sbuf,
    rstat,
    statbuf,
    facbuf,
    zo,
    zro,
    zs,
    zrs,
    newk,
    nstat,
    nadd,
    fin,
    cache_sem,
    tab_sem,
    above,
    across,
    zq_s,
    zq_r,
    q_s,
    q_r1,
    q_r2,
    o_s,
    o_r,
    st_s,
    st_r,
    zo_s,
    zo_r,
    zs_s,
    zs_r,
):
    KVL = max(1, KVH // T)
    HB = H // T
    HU = HB // KVL
    R = STEPS * HU
    LW = BATCH * R
    SW = 2 * KVL
    NB = 1 + G // BATCH
    pos = res.shape[1]
    half = KVH * HD
    g = lax.axis_index("group")
    t = lax.axis_index("tensor")
    offset = t * pos

    def peer_t(k):
        return lax.rem(t + k, T)

    paired = G & (G - 1) == 0
    relay = T == 4
    row_dev = t + 1 - 2 * lax.rem(t, 2)
    col_dev = t + 2 - 4 * lax.div(t, 2)
    greeted = (row_dev, col_dev, T - 1 - t) if relay else [lax.rem(t + n, T) for n in range(1, T)]

    ways = list(dict.fromkeys((2, 3, G - 2, G - 1, *range(4, G), 1, 0)))
    mine, beside = G - 1, G - 2

    def peer_g(k):
        return flipped(g, ways[k]) if paired else lax.rem(g + ways[k], G)

    def from_g(k):
        return peer_g(k) if paired else lax.rem(g - ways[k] + G, G)

    def over_t(src, dst, ssem, rsem, dev):
        return pltpu.make_async_remote_copy(
            src_ref=src, dst_ref=dst, send_sem=ssem, recv_sem=rsem,
            device_id=(g, dev), device_id_type=MESH,
        )

    def over_g(src, dst, ssem, rsem, dev):
        return pltpu.make_async_remote_copy(
            src_ref=src, dst_ref=dst, send_sem=ssem, recv_sem=rsem,
            device_id=(dev, t), device_id_type=MESH,
        )

    def c_zq(k):
        return over_g(zq.at[k], qall.at[t, RES_DEV + k], zq_s.at[0], zq_r.at[k], peer_g(k))

    def relayed(s):
        return relay and (s < RES_DEV or s - RES_DEV in (mine, beside))

    def send_own(s):
        own = qall.at[t, s]
        if not relayed(s):
            for dev in greeted:
                over_t(own, own, q_s.at[0], q_r2.at[s], dev).start()
            return
        rows, cols = (q_r1, q_r2) if s % 2 == 0 else (q_r2, q_r1)
        over_t(own, own, q_s.at[0], rows.at[s], row_dev).start()
        over_t(own, own, q_s.at[0], cols.at[s], col_dev).start()

    def pass_on(s):
        if not relayed(s):
            return
        near, far = (row_dev, col_dev) if s % 2 == 0 else (col_dev, row_dev)
        one = qall.at[near, s]
        over_t(one, one, q_s.at[0], q_r1.at[s], far).wait_recv()
        over_t(one, one, q_s.at[0], q_r2.at[s], far).start()

    def whole(s, came):
        rest = qall.at[pl.ds(0, came), s]
        over_t(rest, rest, q_s.at[0], q_r2.at[s], t).wait_recv()

    def c_o(b, j, n):
        p = peer_t(n)
        rows = pl.ds(pl.multiple_of(j * R, R), R)
        return over_t(
            obuf.at[b, p, :, rows], rbuf.at[b, n, :, rows], o_s.at[b], o_r.at[b], p
        )

    def c_st(b, n):
        p = peer_t(n)
        return over_t(sbuf.at[b, p], rstat.at[b, n], st_s.at[b], st_r.at[b], p)

    def c_zo(k):
        return over_g(zo.at[k], zro.at[k], zo_s.at[0], zo_r.at[k // BATCH], from_g(k))

    def c_zs(k):
        return over_g(zs.at[k // BATCH], zrs.at[k], zs_s.at[0], zs_r.at[k // BATCH], from_g(k))

    barrier = pltpu.get_barrier_semaphore()
    moving = [k for k in range(G) if k != mine]

    def when_above(k, act):
        @pl.when(peer_g(k) > g)
        def _():
            act()

    def when_below(k, act):
        @pl.when(peer_g(k) < g)
        def _():
            act()

    def greet(k):
        pl.semaphore_signal(barrier, inc=1, device_id=(peer_g(k), t), device_id_type=MESH)

    def answer(k):
        back = k if paired else ways.index((G - ways[k]) % G)
        pl.semaphore_signal(
            above.at[back], inc=1, device_id=(peer_g(k), t), device_id_type=MESH
        )

    def send_up(k):
        pl.semaphore_wait(above.at[k], 1)
        c_zq(k).start()

    def late(k):
        when_above(k, functools.partial(send_up, k))

    def meet():
        pl.semaphore_wait(barrier, g + (2 if relay else T - 1))
        for k in moving:
            when_below(k, functools.partial(answer, k))
        if relay:
            pl.semaphore_signal(
                across.at[0], inc=1, device_id=(g, row_dev), device_id_type=MESH
            )

    for k in moving:
        when_above(k, functools.partial(greet, k))
    for dev in greeted[:2] if relay else greeted:
        pl.semaphore_signal(barrier, inc=1, device_id=(g, dev), device_id_type=MESH)
    load_q = pltpu.make_async_copy(q_hbm, q_in, cache_sem.at[2])
    load_new = pltpu.make_async_copy(new_hbm, new_in, cache_sem.at[3])
    load_res = pltpu.make_async_copy(res_hbm, res, cache_sem.at[0])
    load_pre = pltpu.make_async_copy(pre_hbm, pre, cache_sem.at[1])
    tables = [
        pltpu.make_async_copy(src, dst, tab_sem.at[i])
        for i, (src, dst) in enumerate(
            ((kept_hbm, kept_v), (home_hbm, home_v), (dest_hbm, dest_v), (stay_hbm, kept))
        )
    ]
    for copy in tables:
        copy.start()
    load_q.start()
    load_new.start()
    load_q.wait()
    for row in range(PER_GROUP):
        for h in range(HB):
            piece = q_in[row, :, h * HD : (h + 1) * HD]
            stage[row, h * STEPS : (h + 1) * STEPS, :] = piece.astype(F32)
    for j in range(RES_DEV):
        qall[t, j] = stage[j].astype(BF16)
    meet()
    for j in range(RES_DEV):
        send_own(j)
    for copy in tables:
        copy.wait()
    load_pre.start()
    load_res.start()
    sources = [from_g(k) for k in range(G)]
    fill_table([peer_g(k) for k in range(G)], sources, g, kept_v, home_v, dest_v, tab_v)
    load_tab = pltpu.make_async_copy(tab_v, tab_s, cache_sem.at[4])
    load_tab.start()
    load_tab.wait()

    for k in range(G):
        block = stage[tab_s[k, 0]].astype(BF16)
        zq[k] = block
        if k == mine:
            qall[t, RES_DEV + k] = block

    send_own(RES_DEV + mine)
    for k in moving:
        when_below(k, c_zq(k).start)

    kv_col = pl.multiple_of((t * KVL * KVH) // (T * KVL) * HD, HD)

    def stage_new(b):
        for j in range(BATCH):
            row = j if b == 0 else tab_s[(b - 1) * BATCH + j, 0]
            lo = j * STEPS
            newk[b, 0, lo : lo + STEPS, :] = new_in[row, :, pl.ds(kv_col, KVL * HD)].astype(F32)
            newk[b, 1, lo : lo + STEPS, :] = new_in[
                row, :, pl.ds(pl.multiple_of(half + kv_col, HD), KVL * HD)
            ].astype(F32)

    def queries_of(b):
        return [
            jnp.concatenate(
                [
                    (qall[t, j] if b == 0 else zq[(b - 1) * BATCH + j])[i * R : (i + 1) * R]
                    for j in range(BATCH)
                ],
                axis=0,
            )
            for i in range(KVL)
        ]

    r16 = lax.broadcasted_iota(jnp.int32, (BATCH * STEPS, LW), 0)
    lanes16 = lax.broadcasted_iota(jnp.int32, (BATCH * STEPS, LW), 1)
    causal = (r16 // STEPS == lanes16 // R) & (r16 % STEPS <= lanes16 % STEPS)
    def fresh(b):
        stage_new(b)
        asked_b = queries_of(b)
        for i in range(KVL):
            keys = newk[b, 0, :, i * HD : (i + 1) * HD].astype(BF16)
            values = newk[b, 1, :, i * HD : (i + 1) * HD].astype(BF16)
            scores = lax.dot_general(keys, asked_b[i], NT, preferred_element_type=F32) * SCALE
            scores = jnp.where(causal, scores, NEG_FLOOR)
            top = jnp.max(scores, axis=0, keepdims=True)
            weights = jnp.where(causal, jnp.exp(scores - top), 0.0)
            nstat[b, i : i + 1, :] = top
            nstat[b, KVL + i : KVL + i + 1, :] = jnp.sum(weights, axis=0, keepdims=True)
            nadd[b, i] = lax.dot_general(
                weights.astype(BF16), values, TN, preferred_element_type=F32
            )


    def forward(k):
        c_zq(k).wait_recv()
        send_own(RES_DEV + k)

    def attend_slot(cache, row, length, slot, b, j, hold=False):
        lane = lax.broadcasted_iota(jnp.int32, (R, 128), 1)
        usable = offset + lax.broadcasted_iota(jnp.int32, (R, pos), 1) < length
        stat = jnp.zeros((R, 128), F32)
        rows = pl.ds(pl.multiple_of(j * R, R), R)
        W = 2 if KVL % 2 == 0 else 1
        units = [(tt, i) for tt in range(T) for i in range(0, KVL, W)]
        all_scores = []
        for tt, i in units:
            kv = (tt * KVL + i) * KVH // (T * KVL)
            asked = qall[tt, slot, i * R : (i + W) * R, :]
            keys = jnp.concatenate(
                [cache[row, :, (kv + w) * HD : (kv + w + 1) * HD] for w in range(W)], axis=0
            )
            scores = lax.dot_general(asked, keys, NT, preferred_element_type=F32)
            all_scores.append(
                [scores[w * R : (w + 1) * R, w * pos : (w + 1) * pos] * SCALE for w in range(W)]
            )
        all_weights = []
        for (tt, i), scores in zip(units, all_scores):
            rounded = []
            for w in range(W):
                masked = jnp.where(usable, scores[w], NEG_FLOOR)
                highest = jnp.max(masked, axis=1, keepdims=True)
                weights = jnp.where(usable, jnp.exp(masked - highest), 0.0)
                total = jnp.sum(weights, axis=1, keepdims=True)
                rounded.append(weights.astype(BF16))
                stat = jnp.where(lane == tt * SW + i + w, highest, stat)
                stat = jnp.where(lane == tt * SW + KVL + i + w, total, stat)
            all_weights.append(jnp.concatenate(rounded, axis=0))
        for (tt, i), weights in zip(units, all_weights):
            kv = (tt * KVL + i) * KVH // (T * KVL)
            values = cache[row, :, half + kv * HD : half + (kv + W) * HD]
            blended = jnp.dot(weights, values, preferred_element_type=F32)
            for w in range(W):
                obuf[b, tt, i + w, rows, :] = blended[
                    w * R : (w + 1) * R, w * HD : (w + 1) * HD
                ].astype(BF16)
        statbuf[rows, :] = stat
        if not hold:
            for n in range(1, T):
                c_o(b, j, n).start()

    def send_stats(b):
        for n in range(1, T):
            c_st(b, n).start()
        rbuf[b, 0] = obuf[b, t]
        rstat[b, 0] = sbuf[b, t]

    rest = pl.ds(1, T - 1)

    def loaded(_):
        load_pre.wait()
        load_res.wait()

    few = 2 if relay else T - 1

    def stay_slots(first, last, hold):
        @pl.loop(first, last)
        def _(j):
            whole(j, few)
            attend_slot(res, j, kept[0, g * RES_DEV + j], j, 0, j, hold)

    def moved_slots(b, first, last, came):
        @pl.loop(first, last)
        def _(j):
            k = (b - 1) * BATCH + j
            whole(RES_DEV + k, came)
            held = tab_s[G + k, 0]
            attend_slot(pre, held % MIG_DEV, held // MIG_DEV, RES_DEV + k, b, j)

    def turn_stats(b):
        turned = statbuf[...].T
        for tt in range(T):
            sbuf[b, tt] = turned[tt * SW : tt * SW + 8, :]

    def attend_batch(b):
        moved_slots(b, 0, BATCH, T - 1)
        turn_stats(b)
        send_stats(b)

    def attend_first(_):
        attend_batch(1)

    def attend_rest(_):
        if NB > 3:
            pl.loop(2, NB - 1)(attend_batch)
        moved_slots(NB - 1, 0, BATCH - 2, T - 1)
        moved_slots(NB - 1, BATCH - 2, BATCH, few)
        turn_stats(NB - 1)
        send_stats(NB - 1)

    def send_stays(_):
        for j in range(RES_DEV):
            for n in range(1, T):
                c_o(0, j, n).start()
        send_stats(0)

    def passing(k):
        pass_on(RES_DEV + k)

    F, W, N, L, PS = forward, passing, fresh, late, pass_on
    load_new.wait()
    middle = list(range(4, beside))
    def reach(_):
        if relay:
            pl.semaphore_wait(across.at[0], 1)

    plan = [(L, beside), (N, 0), (L, 0), (L, 1), (F, beside), (N, 1)]
    plan += [(PS, j) for j in range(RES_DEV)] + [(W, mine)]
    plan += [(L, k) for k in middle] + [(reach, 0), (L, 2), (L, 3)]
    plan += [(F, 0), (F, 1), (W, beside)] + [(F, k) for k in middle] + [(F, 2), (F, 3)] + [(N, b) for b in range(2, NB)] + [(loaded, 0), (lambda _: stay_slots(0, RES_DEV, True), 0)]
    plan += [(turn_stats, 0), (attend_first, 0), (attend_rest, 0), (send_stays, 0)]
    for step, p in plan:
        step(p)

    def merged(b):
        over_t(rstat.at[b, rest], rstat.at[b, rest], st_s.at[b], st_r.at[b], t).wait_recv()
        over_t(rbuf.at[b, rest], rbuf.at[b, rest], o_s.at[b], o_r.at[b], t).wait_recv()
        tops = [rstat[b, n][:KVL] for n in range(T)]
        highest = functools.reduce(jnp.maximum, tops)
        total = jnp.zeros((KVL, LW), F32)
        for n in range(T):
            factor = jnp.exp(tops[n] - highest)
            total = total + factor * rstat[b, n][KVL:SW]
            facbuf[n * KVL : (n + 1) * KVL, :] = factor
        columns = facbuf[...].T
        blended = []
        for i in range(KVL):
            sum_i = jnp.zeros((LW, HD), F32)
            for n in range(T):
                c = n * KVL + i
                sum_i = sum_i + rbuf[b, n, i].astype(F32) * columns[:, c : c + 1]
            blended.append(sum_i)
        return highest, total, blended

    def finish(b, highest, total, blended):
        new_top, new_total = nstat[b, 0:KVL], nstat[b, KVL:SW]
        top = jnp.maximum(highest, new_top)
        old_part, new_part = jnp.exp(highest - top), jnp.exp(new_top - top)
        inverse = 1.0 / (total * old_part + new_total * new_part)
        facbuf[0:KVL, :] = old_part * inverse
        facbuf[KVL:SW, :] = new_part * inverse
        columns = facbuf[...].T
        for i in range(KVL):
            done = blended[i] * columns[:, i : i + 1]
            done = done + nadd[b, i] * columns[:, KVL + i : KVL + i + 1]
            for j in range(BATCH):
                fin[b * BATCH + j, i * R : (i + 1) * R, :] = done[j * R : (j + 1) * R]

    def put(slot, row):
        for h in range(HB):
            piece = fin[slot, h * STEPS : (h + 1) * STEPS, :]
            out[row, :, h * HD : (h + 1) * HD] = piece.astype(BF16)

    for b in range(1, NB):
        highest, total, blended = merged(b)
        packed = jnp.concatenate([highest, total], axis=0)
        zs[b - 1, 0:SW, :] = packed
        for j in range(BATCH):
            k = (b - 1) * BATCH + j
            for i in range(KVL):
                zo[k, i] = blended[i][j * R : (j + 1) * R].astype(BF16)
            if k != mine:
                c_zs(k).start()
                c_zo(k).start()
            else:
                zrs[k] = zs[b - 1]
                zro[k] = zo[k]

    finish(0, *merged(0))
    for j in range(RES_DEV):
        put(j, j)

    for b in range(1, NB):
        lanes = lax.broadcasted_iota(jnp.int32, (8, LW), 1)
        stats = jnp.zeros((8, LW), F32)
        first = (b - 1) * BATCH
        came = pl.ds(first, BATCH - (first <= mine < first + BATCH))
        over_g(zrs.at[came], zrs.at[came], zs_s.at[0], zs_r.at[b - 1], g).wait_recv()
        over_g(zro.at[came], zro.at[came], zo_s.at[0], zo_r.at[b - 1], g).wait_recv()
        for j in range(BATCH):
            k = (b - 1) * BATCH + j
            stats = jnp.where(lanes // R == j, zrs[k], stats)
        blended = [
            jnp.concatenate(
                [zro[(b - 1) * BATCH + j, i].astype(F32) for j in range(BATCH)], axis=0
            )
            for i in range(KVL)
        ]
        finish(b, stats[:KVL], stats[KVL:SW], blended)
    for l in range(MIG_DEV):
        k_of = 0
        for k in range(G):
            k_of = jnp.where(tab_s[k, 0] == RES_DEV + l, k, k_of)
        put(RES_DEV + k_of, RES_DEV + l)

    others = pl.ds(1, G - 1)
    over_g(zq.at[others], zq.at[others], zq_s.at[0], zq_r.at[0], g).wait_send()
    over_g(zrs.at[others], zrs.at[others], zs_s.at[0], zs_r.at[0], g).wait_send()
    over_g(zo.at[others], zo.at[others], zo_s.at[0], zo_r.at[0], g).wait_send()
    sent = qall.at[pl.ds(0, T - 1)]
    over_t(sent, sent, q_s.at[0], q_r2.at[0], t).wait_send()
    for b in range(NB):
        over_t(rstat.at[b, rest], rstat.at[b, rest], st_s.at[b], st_r.at[b], t).wait_send()
        over_t(rbuf.at[b, rest], rbuf.at[b, rest], o_s.at[b], o_r.at[b], t).wait_send()


def body(
    queries,
    new_entries,
    resident_cache,
    prefill_cache,
    resident_kept,
    kept_tokens,
    prefill_slot,
    decode_slot,
):
    G = lax.axis_size("group")
    T = lax.axis_size("tensor")
    KVL = max(1, KVH // T)
    HB = H // T
    RB = STEPS * HB
    R = RB // KVL
    LW = BATCH * R
    NB = 1 + G // BATCH
    dma = pltpu.SemaphoreType.DMA
    vmem = pl.BlockSpec(memory_space=pltpu.VMEM)
    hbm = pl.BlockSpec(memory_space=pl.ANY)
    return pl.pallas_call(
        functools.partial(kernel, G, T),
        out_shape=pltpu.VMEM(queries.shape, BF16),
        in_specs=[hbm] * 8,
        out_specs=vmem,
        scratch_shapes=[
            pltpu.VMEM((1, kept_tokens.shape[0]), jnp.int32),
            pltpu.VMEM((1, prefill_slot.shape[0]), jnp.int32),
            pltpu.VMEM((1, decode_slot.shape[0]), jnp.int32),
            pltpu.SMEM((1, resident_kept.shape[0]), jnp.int32),
            pltpu.VMEM((2 * G, 128), jnp.int32),
            pltpu.SMEM((2 * G, 128), jnp.int32),
            pltpu.VMEM(queries.shape, BF16),
            pltpu.VMEM(new_entries.shape, BF16),
            pltpu.VMEM(resident_cache.shape, BF16),
            pltpu.VMEM(prefill_cache.shape, BF16),
            pltpu.VMEM((T, RES_DEV + G, RB, HD), BF16),
            pltpu.VMEM((G, RB, HD), BF16),
            pltpu.VMEM((PER_GROUP, RB, HD), F32),
            pltpu.VMEM((NB, T, KVL, LW, HD), BF16),
            pltpu.VMEM((NB, T, KVL, LW, HD), BF16),
            pltpu.VMEM((NB, T, 8, LW), F32),
            pltpu.VMEM((NB, T, 8, LW), F32),
            pltpu.VMEM((LW, 128), F32),
            pltpu.VMEM((128, LW), F32),
            pltpu.VMEM((G, KVL, R, HD), BF16),
            pltpu.VMEM((G, KVL, R, HD), BF16),
            pltpu.VMEM((NB - 1, 8, LW), F32),
            pltpu.VMEM((G, 8, LW), F32),
            pltpu.VMEM((NB, 2, BATCH * STEPS, KVL * HD), F32),
            pltpu.VMEM((NB, 8, LW), F32),
            pltpu.VMEM((NB, KVL, LW, HD), F32),
            pltpu.VMEM((NB * BATCH, RB, HD), F32),
            dma((5,)),
            dma((4,)),
            pltpu.SemaphoreType.REGULAR((G,)),
            pltpu.SemaphoreType.REGULAR((1,)),
            dma((1,)),
            dma((G,)),
            dma((1,)),
            dma((RES_DEV + G,)),
            dma((RES_DEV + G,)),
            dma((NB,)),
            dma((NB,)),
            dma((NB,)),
            dma((NB,)),
            dma((1,)),
            dma((NB - 1,)),
            dma((1,)),
            dma((NB - 1,)),
        ],
        compiler_params=pltpu.CompilerParams(collective_id=0, has_side_effects=True),
    )(
        kept_tokens[None],
        prefill_slot[None],
        decode_slot[None],
        resident_kept[None],
        queries, new_entries, resident_cache, prefill_cache)


def solution(mesh):
    in_specs = (
        P("group", None, "tensor"),
        P("group", None, None),
        P("group", "tensor", None),
        P("group", "tensor", None),
        P(),
        P(),
        P(),
        P(),
    )
    out_specs = P("group", None, "tensor")
    return jax.shard_map(body, mesh=mesh, in_specs=in_specs, out_specs=out_specs, check_vma=False)
```

```python
import functools
import math

import jax
import jax.numpy as jnp
from jax import lax
from jax.experimental import pallas as pl
from jax.experimental.pallas import tpu as pltpu
from jax.sharding import PartitionSpec as P

H = 64
KVH = 8
HD = 128
STEPS = 4
MIG_DEV = 8
RES_DEV = 4
PER_GROUP = RES_DEV + MIG_DEV
BATCH = 2
STAY = RES_DEV // BATCH

NEG_FLOOR = -1e30
SCALE = 1.0 / math.sqrt(HD)
MESH = pl.DeviceIdType.MESH
F32 = jnp.float32
BF16 = jnp.bfloat16
NT = (((1,), (1,)), ((), ()))
TN = (((0,), (0,)), ((), ()))


def flipped(v, mask):
    out, bit = v, 1
    while bit <= mask:
        if mask & bit:
            out = out + bit * (1 - 2 * lax.rem(lax.div(v, bit), 2))
        bit *= 2
    return out


def fill_table(peers, sources, g, kept_v, home_v, dest_v, tab_v):
    G = len(peers)
    shape = (2 * G, dest_v.shape[1])
    n = lax.broadcasted_iota(jnp.int32, shape, 0)
    dest = jnp.broadcast_to(dest_v[...], shape)
    home = jnp.broadcast_to(home_v[...], shape)
    kept = jnp.broadcast_to(kept_v[...], shape)
    dest_group, home_group = lax.div(dest, PER_GROUP), lax.div(home, MIG_DEV)
    other = jnp.zeros(shape, jnp.int32)
    for k in range(G):
        other = jnp.where(n == k, peers[k], other)
        other = jnp.where(n == G + k, sources[k], other)
    arriving = (n < G) & (dest_group == g) & (home_group == other)
    leaving = (n >= G) & (home_group == g) & (dest_group == other)
    picked = jnp.where(arriving, dest - dest_group * PER_GROUP, 0)
    held = home - home_group * MIG_DEV + MIG_DEV * kept
    picked = picked + jnp.where(leaving, held, 0)
    total = jnp.sum(picked, axis=1, keepdims=True)
    tab_v[...] = jnp.broadcast_to(total, tab_v.shape)


def kernel(
    G,
    T,
    kept_hbm,
    home_hbm,
    dest_hbm,
    stay_hbm,
    q_hbm,
    new_hbm,
    res_hbm,
    pre_hbm,
    out,
    kept_v,
    home_v,
    dest_v,
    kept,
    tab_v,
    tab_s,
    q_in,
    new_in,
    res,
    pre,
    qall,
    zq,
    stage,
    obuf,
    rbuf,
    sbuf,
    rstat,
    statbuf,
    facbuf,
    zo,
    zro,
    zs,
    zrs,
    newk,
    nstat,
    nadd,
    fin,
    cache_sem,
    tab_sem,
    above,
    across,
    zq_s,
    zq_r,
    q_s,
    q_r,
    o_s,
    o_r,
    st_s,
    st_r,
    zo_s,
    zo_r,
    zs_s,
    zs_r,
):
    KVL = max(1, KVH // T)
    HB = H // T
    HU = HB // KVL
    R = STEPS * HU
    LW = BATCH * R
    PW = KVL * LW
    NB = STAY + G // BATCH
    pos = res.shape[1]
    half = KVH * HD
    g = lax.axis_index("group")
    t = lax.axis_index("tensor")
    offset = t * pos

    def peer_t(k):
        return lax.rem(t + k, T)

    paired = G & (G - 1) == 0
    square = T == 4
    row_dev = t + 1 - 2 * lax.rem(t, 2)
    col_dev = t + 2 - 4 * lax.div(t, 2)
    greeted = (row_dev, col_dev, T - 1 - t) if square else [lax.rem(t + n, T) for n in range(1, T)]

    far_pairs = G // 2 - 1
    mine, beside = G - 1, G - 2

    def way(k):
        static = isinstance(k, int)
        if static and k >= beside:
            return mine - k
        pair = k // 2 if static else lax.div(k, 2)
        odd = k % 2 if static else lax.rem(k, 2)
        return 2 * (far_pairs - pair) + odd

    def at_way(mask):
        if not paired:
            return lax.rem(g + mask, G)
        out, bit = 0, 1
        while bit < G:
            a = lax.rem(lax.div(g, bit), 2)
            b = mask // bit % 2 if isinstance(mask, int) else lax.rem(lax.div(mask, bit), 2)
            out = out + bit * (a + b - 2 * a * b)
            bit *= 2
        return out

    def peer_g(k):
        return at_way(way(k))

    def from_g(k):
        return peer_g(k) if paired else at_way(G - way(k))

    level = lax.div(g, 2)
    first = far_pairs - lax.max(level, 1)

    def turn(i):
        if not paired:
            return i
        later = i - 1 + jnp.where(i > first, 1, 0)
        return jnp.where(i == 0, first, later)

    def turn_in(i):
        return jnp.where(first == far_pairs - 1, i, turn(i)) if paired else i

    def over_t(src, dst, ssem, rsem, dev):
        return pltpu.make_async_remote_copy(
            src_ref=src, dst_ref=dst, send_sem=ssem, recv_sem=rsem,
            device_id=(g, dev), device_id_type=MESH,
        )

    def over_g(src, dst, ssem, rsem, dev):
        return pltpu.make_async_remote_copy(
            src_ref=src, dst_ref=dst, send_sem=ssem, recv_sem=rsem,
            device_id=(dev, t), device_id_type=MESH,
        )

    def c_zq(k):
        return over_g(zq.at[k], qall.at[t, RES_DEV + k], zq_s.at[0], zq_r.at[k], peer_g(k))

    near = greeted[:2] if square else greeted

    def send_own(s, devs):
        own = qall.at[t, s]
        for dev in devs:
            over_t(own, own, q_s.at[0], q_r.at[s], dev).start()

    def whole(s):
        rest = qall.at[pl.ds(0, T - 1), s]
        over_t(rest, rest, q_s.at[0], q_r.at[s], t).wait_recv()

    def c_o(b, j, n):
        p = peer_t(n)
        rows = pl.ds(pl.multiple_of(j * R, R), R)
        return over_t(
            obuf.at[b, p, :, rows], rbuf.at[b, n, :, rows], o_s.at[0], o_r.at[b], p
        )

    def c_st(b, n):
        p = peer_t(n)
        return over_t(sbuf.at[b, p], rstat.at[b, n], st_s.at[0], st_r.at[b], p)

    barrier = pltpu.get_barrier_semaphore()
    moving = [k for k in range(G) if k != mine]

    def when_above(k, act):
        @pl.when(peer_g(k) > g)
        def _():
            act()

    def when_below(k, act):
        @pl.when(peer_g(k) < g)
        def _():
            act()

    def greet(k):
        pl.semaphore_signal(barrier, inc=1, device_id=(peer_g(k), t), device_id_type=MESH)

    def answer(k):
        back = k if paired else [way(m) for m in range(G)].index((G - way(k)) % G)
        pl.semaphore_signal(
            above.at[back], inc=1, device_id=(peer_g(k), t), device_id_type=MESH
        )

    def send_up(k):
        pl.semaphore_wait(above.at[k], 1)
        c_zq(k).start()

    def late(k):
        when_above(k, functools.partial(send_up, k))

    def meet():
        pl.semaphore_wait(barrier, g + len(near))
        for k in moving:
            when_below(k, functools.partial(answer, k))
        if square:
            pl.semaphore_signal(
                across.at[0], inc=1, device_id=(g, row_dev), device_id_type=MESH
            )

    for k in moving:
        when_above(k, functools.partial(greet, k))
    for dev in near:
        pl.semaphore_signal(barrier, inc=1, device_id=(g, dev), device_id_type=MESH)
    load_q = pltpu.make_async_copy(q_hbm, q_in, cache_sem.at[2])
    load_new = pltpu.make_async_copy(new_hbm, new_in, cache_sem.at[3])
    load_res = pltpu.make_async_copy(res_hbm, res, cache_sem.at[0])
    load_pre = pltpu.make_async_copy(pre_hbm, pre, cache_sem.at[1])
    tables = [
        pltpu.make_async_copy(src, dst, tab_sem.at[i])
        for i, (src, dst) in enumerate(
            ((kept_hbm, kept_v), (home_hbm, home_v), (dest_hbm, dest_v), (stay_hbm, kept))
        )
    ]
    for copy in tables:
        copy.start()
    load_q.start()
    load_new.start()
    load_q.wait()
    for row in range(PER_GROUP):
        for h in range(HB):
            piece = q_in[row, :, h * HD : (h + 1) * HD]
            stage[row, h * STEPS : (h + 1) * STEPS, :] = piece.astype(F32)
    for j in range(RES_DEV):
        qall[t, j] = stage[j].astype(BF16)
    meet()
    for j in range(RES_DEV):
        send_own(j, near)
    for copy in tables:
        copy.wait()
    load_pre.start()
    load_res.start()
    sources = [from_g(k) for k in range(G)]
    fill_table([peer_g(k) for k in range(G)], sources, g, kept_v, home_v, dest_v, tab_v)
    load_tab = pltpu.make_async_copy(tab_v, tab_s, cache_sem.at[4])
    load_tab.start()
    load_tab.wait()

    for k in range(G):
        block = stage[tab_s[k, 0]].astype(BF16)
        zq[k] = block
        if k == mine:
            qall[t, RES_DEV + k] = block

    for k in reversed(moving):
        when_below(k, c_zq(k).start)
    send_own(RES_DEV + mine, near)

    kv_col = pl.multiple_of((t * KVL * KVH) // (T * KVL) * HD, HD)

    def stage_new(b):
        for j in range(BATCH):
            row = b * BATCH + j if b < STAY else tab_s[(b - STAY) * BATCH + j, 0]
            for c in range(2):
                for i in range(KVL):
                    lo = (i * BATCH + j) * STEPS
                    col = pl.multiple_of(c * half + kv_col + i * HD, HD)
                    newk[b, c, lo : lo + STEPS, :] = new_in[row, :, pl.ds(col, HD)].astype(F32)

    def asked_of(b, j):
        return qall[t, b * BATCH + j] if b < STAY else zq[(b - STAY) * BATCH + j]

    r16 = lax.broadcasted_iota(jnp.int32, (KVL * BATCH * STEPS, PW), 0)
    lanes16 = lax.broadcasted_iota(jnp.int32, (KVL * BATCH * STEPS, PW), 1)
    causal = (r16 // STEPS == lanes16 // R) & (r16 % STEPS <= lanes16 % STEPS)

    def fresh(b):
        stage_new(b)
        asked = jnp.concatenate(
            [asked_of(b, j)[i * R : (i + 1) * R] for i in range(KVL) for j in range(BATCH)],
            axis=0,
        )
        keys, values = newk[b, 0].astype(BF16), newk[b, 1].astype(BF16)
        scores = lax.dot_general(keys, asked, NT, preferred_element_type=F32) * SCALE
        scores = jnp.where(causal, scores, NEG_FLOOR)
        top = jnp.max(scores, axis=0, keepdims=True)
        weights = jnp.where(causal, jnp.exp(scores - top), 0.0)
        nstat[b, 0:1, :] = top
        nstat[b, 1:2, :] = jnp.sum(weights, axis=0, keepdims=True)
        nadd[b] = lax.dot_general(
            weights.astype(BF16), values, TN, preferred_element_type=F32
        )

    def forward(k):
        came = qall.at[t, RES_DEV + k]
        over_g(came, came, zq_s.at[0], zq_r.at[k], g).wait_recv()
        send_own(RES_DEV + k, greeted)

    def attend_slot(cache, row, length, slot, b, j, hold=False):
        lane = lax.broadcasted_iota(jnp.int32, (R, 128), 1)
        usable = offset + lax.broadcasted_iota(jnp.int32, (R, pos), 1) < length
        stats = [jnp.zeros((R, 128), F32) for _ in range(KVL)]
        rows = pl.ds(pl.multiple_of(j * R, R), R)
        W = 2 if KVL % 2 == 0 else 1
        units = [(tt, i) for tt in range(T) for i in range(0, KVL, W)]
        all_scores = []
        for tt, i in units:
            kv = (tt * KVL + i) * KVH // (T * KVL)
            asked = qall[tt, slot, i * R : (i + W) * R, :]
            keys = jnp.concatenate(
                [cache[row, :, (kv + w) * HD : (kv + w + 1) * HD] for w in range(W)], axis=0
            )
            scores = lax.dot_general(asked, keys, NT, preferred_element_type=F32)
            all_scores.append(
                [scores[w * R : (w + 1) * R, w * pos : (w + 1) * pos] * SCALE for w in range(W)]
            )
        all_weights = []
        for (tt, i), scores in zip(units, all_scores):
            rounded = []
            for w in range(W):
                masked = jnp.where(usable, scores[w], NEG_FLOOR)
                highest = jnp.max(masked, axis=1, keepdims=True)
                weights = jnp.where(usable, jnp.exp(masked - highest), 0.0)
                total = jnp.sum(weights, axis=1, keepdims=True)
                rounded.append(weights.astype(BF16))
                stats[i + w] = jnp.where(lane == 2 * tt, highest, stats[i + w])
                stats[i + w] = jnp.where(lane == 2 * tt + 1, total, stats[i + w])
            all_weights.append(jnp.concatenate(rounded, axis=0))
        for (tt, i), weights in zip(units, all_weights):
            kv = (tt * KVL + i) * KVH // (T * KVL)
            values = cache[row, :, half + kv * HD : half + (kv + W) * HD]
            blended = jnp.dot(weights, values, preferred_element_type=F32)
            for w in range(W):
                obuf[b, tt, i + w, rows, :] = blended[
                    w * R : (w + 1) * R, w * HD : (w + 1) * HD
                ].astype(BF16)
        for i in range(KVL):
            statbuf[pl.ds(pl.multiple_of(i * LW + j * R, R), R), :] = stats[i]
        if not hold:
            for n in range(1, T):
                c_o(b, j, n).start()

    def send_stats(b):
        for n in range(1, T):
            c_st(b, n).start()
        rbuf[b, 0] = obuf[b, t]
        rstat[b, 0] = sbuf[b, t]

    rest = pl.ds(1, T - 1)

    def loaded(_):
        load_pre.wait()
        load_res.wait()

    def turn_stats(b):
        turned = statbuf[...].T
        for tt in range(T):
            sbuf[b, tt] = turned[2 * tt : 2 * tt + 2, :]

    def stay_batch(b, hold=True):
        @pl.loop(0, BATCH)
        def _(j):
            s = b * BATCH + j
            whole(s)
            attend_slot(res, s, kept[0, g * RES_DEV + s], s, b, j, hold)

        turn_stats(b)
        if not hold:
            send_stats(b)

    def moved_batch(b, hold=False):
        @pl.loop(0, BATCH)
        def _(j):
            k = (b - STAY) * BATCH + j
            whole(RES_DEV + k)
            held = tab_s[G + k, 0]
            attend_slot(pre, held % MIG_DEV, held // MIG_DEV, RES_DEV + k, b, j, hold)

        turn_stats(b)
        if not hold:
            send_stats(b)

    def send_batch(b):
        for j in range(BATCH):
            for n in range(1, T):
                c_o(b, j, n).start()
        send_stats(b)

    def reach(_):
        if square:
            pl.semaphore_wait(across.at[0], 1)
            for s in (*range(RES_DEV), RES_DEV + mine):
                send_own(s, greeted[2:])

    def stays():
        pl.loop(0, STAY)(stay_batch)

    def locals_held(_):
        moved_batch(NB - 1, True)

    def far(_):
        @pl.loop(0, far_pairs)
        def _(i):
            moved_batch(STAY + turn(i))

    def forward_far(_):
        @pl.loop(0, far_pairs - 1)
        def _(i):
            for j in range(2):
                forward(2 * turn_in(i) + j)


    F, N, L = forward, fresh, late
    load_new.wait()
    middle = list(range(2, beside))
    early = g < G // 4

    def stays_early(_):
        @pl.when(early)
        def _():
            stay_batch(0, False)
            pl.loop(1, STAY)(stay_batch)

    def stays_late(_):
        pl.when(jnp.logical_not(early))(stays)

    def held_late(_):
        pl.when(jnp.logical_not(early))(functools.partial(send_batch, 0))
        for b in range(1, STAY):
            send_batch(b)

    plan = [(L, beside), (N, 0), (L, beside - 2), (L, beside - 1), (reach, 0), (F, beside)]
    plan += [(N, 1)] + [(L, k) for k in reversed(range(beside - 2))]
    plan += [(F, beside - 2), (F, beside - 1), (loaded, 0), (stays_early, 0), (N, NB - 1)]
    plan += [(forward_far, 0)]
    plan += [(stays_late, 0), (locals_held, 0), (far, 0), (send_batch, NB - 1)]
    plan += [(held_late, 0)]
    plan += [(N, b) for b in range(STAY, NB - 1)]
    for step, p in plan:
        step(p)

    def arrived(b):
        over_t(rstat.at[b, rest], rstat.at[b, rest], st_s.at[0], st_r.at[b], t).wait_recv()
        over_t(rbuf.at[b, rest], rbuf.at[b, rest], o_s.at[0], o_r.at[b], t).wait_recv()

    def merged(b):
        tops = [rstat[b, n][0:1] for n in range(T)]
        highest = functools.reduce(jnp.maximum, tops)
        total = jnp.zeros((1, PW), F32)
        for n in range(T):
            factor = jnp.exp(tops[n] - highest)
            total = total + factor * rstat[b, n][1:2]
            facbuf[b, n : n + 1, :] = factor
        columns = facbuf[b].T
        blended = jnp.zeros((PW, HD), F32)
        for n in range(T):
            part = rbuf[b, n].reshape(PW, HD).astype(F32)
            blended = blended + part * columns[:, n : n + 1]
        return highest, total, blended

    def finish(b, highest, total, blended):
        new_top, new_total = nstat[b, 0:1], nstat[b, 1:2]
        top = jnp.maximum(highest, new_top)
        old_part, new_part = jnp.exp(highest - top), jnp.exp(new_top - top)
        inverse = 1.0 / (total * old_part + new_total * new_part)
        facbuf[NB + b, 0:1, :] = old_part * inverse
        facbuf[NB + b, 1:2, :] = new_part * inverse
        columns = facbuf[NB + b].T
        done = blended * columns[:, 0:1] + nadd[b] * columns[:, 1:2]
        for j in range(BATCH):
            for i in range(KVL):
                lo = i * LW + j * R
                fin[b * BATCH + j, i * R : (i + 1) * R, :] = done[lo : lo + R]

    def put(slot, row):
        for h in range(HB):
            piece = fin[slot, h * STEPS : (h + 1) * STEPS, :]
            out[row, :, h * HD : (h + 1) * HD] = piece.astype(BF16)

    def give_back(b):
        arrived(b)
        highest, total, blended = merged(b)
        zs[b - STAY] = jnp.concatenate([highest, total], axis=0)
        for j in range(BATCH):
            k = (b - STAY) * BATCH + j
            for i in range(KVL):
                zo[k, i] = blended[i * LW + j * R : i * LW + (j + 1) * R].astype(BF16)
            if isinstance(k, int) and k == mine:
                zrs[k] = zs[b - STAY]
                zro[k] = zo[k]
            else:
                pair, dev = b - STAY, from_g(k)
                over_g(zs.at[pair], zrs.at[k], zs_s.at[0], zs_r.at[pair], dev).start()
                over_g(zo.at[k], zro.at[k], zo_s.at[0], zo_r.at[pair], dev).start()

    def give_far(_):
        @pl.loop(0, far_pairs)
        def _(i):
            give_back(STAY + turn(i))

    def end_stay(b):
        finish(b, *merged(b))
        for j in range(BATCH):
            put(b * BATCH + j, b * BATCH + j)

    def returned(b):
        first = (b - STAY) * BATCH
        came = pl.ds(first, BATCH - (first <= mine < first + BATCH))
        over_g(zrs.at[came], zrs.at[came], zs_s.at[0], zs_r.at[b - STAY], g).wait_recv()
        over_g(zro.at[came], zro.at[came], zo_s.at[0], zo_r.at[b - STAY], g).wait_recv()

    def end_moved(b):
        lanes = lax.broadcasted_iota(jnp.int32, (2, PW), 1)
        stats = jnp.zeros((2, PW), F32)
        first = (b - STAY) * BATCH
        for j in range(BATCH):
            stats = jnp.where((lanes // R) % BATCH == j, zrs[first + j], stats)
        blended = jnp.concatenate(
            [zro[first + j, i].astype(F32) for i in range(KVL) for j in range(BATCH)], axis=0
        )
        finish(b, stats[0:1], stats[1:2], blended)

    moved = list(range(STAY, NB))
    def stay_early(_):
        @pl.when(early)
        def _():
            arrived(0)
            end_stay(0)

    def stay_late(_):
        @pl.when(jnp.logical_not(early))
        def _():
            arrived(0)
            end_stay(0)

    plan = [(stay_early, 0), (give_far, 0), (give_back, moved[-1]), (stay_late, 0)]
    plan += [(returned, b) for b in moved] + [(end_moved, b) for b in moved]
    for b in range(1, STAY):
        plan += [(arrived, b), (end_stay, b)]
    for step, p in plan:
        step(p)
    for l in range(MIG_DEV):
        k_of = 0
        for k in range(G):
            k_of = jnp.where(tab_s[k, 0] == RES_DEV + l, k, k_of)
        put(RES_DEV + k_of, RES_DEV + l)

    others = pl.ds(1, G - 1)
    over_g(zq.at[others], zq.at[others], zq_s.at[0], zq_r.at[0], g).wait_send()
    over_g(zrs.at[others], zrs.at[others], zs_s.at[0], zs_r.at[0], g).wait_send()
    over_g(zo.at[others], zo.at[others], zo_s.at[0], zo_r.at[0], g).wait_send()
    sent = qall.at[pl.ds(0, T - 1)]
    over_t(sent, sent, q_s.at[0], q_r.at[0], t).wait_send()
    stats, parts = rstat.at[:, rest], rbuf.at[:, rest]
    over_t(stats, stats, st_s.at[0], st_r.at[0], t).wait_send()
    over_t(parts, parts, o_s.at[0], o_r.at[0], t).wait_send()


def body(
    queries,
    new_entries,
    resident_cache,
    prefill_cache,
    resident_kept,
    kept_tokens,
    prefill_slot,
    decode_slot,
):
    G = lax.axis_size("group")
    T = lax.axis_size("tensor")
    KVL = max(1, KVH // T)
    HB = H // T
    RB = STEPS * HB
    R = RB // KVL
    LW = BATCH * R
    NB = STAY + G // BATCH
    PW = KVL * LW
    dma = pltpu.SemaphoreType.DMA
    vmem = pl.BlockSpec(memory_space=pltpu.VMEM)
    hbm = pl.BlockSpec(memory_space=pl.ANY)
    return pl.pallas_call(
        functools.partial(kernel, G, T),
        out_shape=pltpu.VMEM(queries.shape, BF16),
        in_specs=[hbm] * 8,
        out_specs=vmem,
        scratch_shapes=[
            pltpu.VMEM((1, kept_tokens.shape[0]), jnp.int32),
            pltpu.VMEM((1, prefill_slot.shape[0]), jnp.int32),
            pltpu.VMEM((1, decode_slot.shape[0]), jnp.int32),
            pltpu.SMEM((1, resident_kept.shape[0]), jnp.int32),
            pltpu.VMEM((2 * G, 128), jnp.int32),
            pltpu.SMEM((2 * G, 128), jnp.int32),
            pltpu.VMEM(queries.shape, BF16),
            pltpu.VMEM(new_entries.shape, BF16),
            pltpu.VMEM(resident_cache.shape, BF16),
            pltpu.VMEM(prefill_cache.shape, BF16),
            pltpu.VMEM((T, RES_DEV + G, RB, HD), BF16),
            pltpu.VMEM((G, RB, HD), BF16),
            pltpu.VMEM((PER_GROUP, RB, HD), F32),
            pltpu.VMEM((NB, T, KVL, LW, HD), BF16),
            pltpu.VMEM((NB, T, KVL, LW, HD), BF16),
            pltpu.VMEM((NB, T, 2, PW), F32),
            pltpu.VMEM((NB, T, 2, PW), F32),
            pltpu.VMEM((PW, 128), F32),
            pltpu.VMEM((2 * NB, max(8, T), PW), F32),
            pltpu.VMEM((G, KVL, R, HD), BF16),
            pltpu.VMEM((G, KVL, R, HD), BF16),
            pltpu.VMEM((NB - STAY, 2, PW), F32),
            pltpu.VMEM((G, 2, PW), F32),
            pltpu.VMEM((NB, 2, KVL * BATCH * STEPS, HD), F32),
            pltpu.VMEM((NB, 2, PW), F32),
            pltpu.VMEM((NB, PW, HD), F32),
            pltpu.VMEM((NB * BATCH, RB, HD), F32),
            dma((5,)),
            dma((4,)),
            pltpu.SemaphoreType.REGULAR((G,)),
            pltpu.SemaphoreType.REGULAR((1,)),
            dma((1,)),
            dma((G,)),
            dma((1,)),
            dma((RES_DEV + G,)),
            dma((1,)),
            dma((NB,)),
            dma((1,)),
            dma((NB,)),
            dma((1,)),
            dma((NB - STAY,)),
            dma((1,)),
            dma((NB - STAY,)),
        ],
        compiler_params=pltpu.CompilerParams(collective_id=0, has_side_effects=True),
    )(
        kept_tokens[None],
        prefill_slot[None],
        decode_slot[None],
        resident_kept[None],
        queries, new_entries, resident_cache, prefill_cache)


def solution(mesh):
    in_specs = (
        P("group", None, "tensor"),
        P("group", None, None),
        P("group", "tensor", None),
        P("group", "tensor", None),
        P(),
        P(),
        P(),
        P(),
    )
    out_specs = P("group", None, "tensor")
    return jax.shard_map(body, mesh=mesh, in_specs=in_specs, out_specs=out_specs, check_vma=False)
```

```python
import functools
import math

import jax
import jax.numpy as jnp
from jax import lax
from jax.experimental import pallas as pl
from jax.experimental.pallas import tpu as pltpu
from jax.sharding import PartitionSpec as P

H = 64
KVH = 8
HD = 128
STEPS = 4
MIG_DEV = 8
RES_DEV = 4
PER_GROUP = RES_DEV + MIG_DEV
BATCH = 2
STAY = RES_DEV // BATCH

NEG_FLOOR = -1e30
SCALE = 1.0 / math.sqrt(HD)
MESH = pl.DeviceIdType.MESH
F32 = jnp.float32
BF16 = jnp.bfloat16
NT = (((1,), (1,)), ((), ()))
TN = (((0,), (0,)), ((), ()))


def flipped(v, mask):
    out, bit = v, 1
    while bit <= mask:
        if mask & bit:
            out = out + bit * (1 - 2 * lax.rem(lax.div(v, bit), 2))
        bit *= 2
    return out


def fill_table(peers, sources, g, plan_v, tab_v):
    G = len(peers)
    shape = (2 * G, plan_v.shape[1])
    n = lax.broadcasted_iota(jnp.int32, shape, 0)
    dest = jnp.broadcast_to(plan_v[2:3, :], shape)
    home = jnp.broadcast_to(plan_v[1:2, :], shape)
    kept = jnp.broadcast_to(plan_v[0:1, :], shape)
    dest_group, home_group = lax.div(dest, PER_GROUP), lax.div(home, MIG_DEV)
    other = jnp.zeros(shape, jnp.int32)
    for k in range(G):
        other = jnp.where(n == k, peers[k], other)
        other = jnp.where(n == G + k, sources[k], other)
    arriving = (n < G) & (dest_group == g) & (home_group == other)
    leaving = (n >= G) & (home_group == g) & (dest_group == other)
    picked = jnp.where(arriving, dest - dest_group * PER_GROUP, 0)
    held = home - home_group * MIG_DEV + MIG_DEV * kept
    picked = picked + jnp.where(leaving, held, 0)
    total = jnp.sum(picked, axis=1, keepdims=True)
    tab_v[...] = jnp.broadcast_to(total, tab_v.shape)


def kernel(
    G,
    T,
    kept_hbm,
    home_hbm,
    dest_hbm,
    stay_hbm,
    q_hbm,
    new_hbm,
    res_hbm,
    pre_hbm,
    out,
    plan_v,
    kept,
    tab_v,
    tab_s,
    q_in,
    new_in,
    cache,
    qall,
    zq,
    stage,
    obuf,
    rbuf,
    sbuf,
    rstat,
    statbuf,
    facbuf,
    zo,
    zro,
    zs,
    zrs,
    newk,
    nstat,
    nadd,
    fin,
    load_sem,
    above,
    across,
    zq_s,
    zq_r,
    q_s,
    q_r,
    o_s,
    o_r,
    st_s,
    st_r,
    zo_s,
    zo_r,
    zs_s,
    zs_r,
):
    KVL = max(1, KVH // T)
    HB = H // T
    HU = HB // KVL
    R = STEPS * HU
    LW = BATCH * R
    PW = KVL * LW
    NB = STAY + G // BATCH
    pos = cache.shape[1]
    half = KVH * HD
    g = lax.axis_index("group")
    t = lax.axis_index("tensor")
    offset = t * pos

    paired = G & (G - 1) == 0
    square = T == 4
    row_dev = t + 1 - 2 * lax.rem(t, 2)
    col_dev = t + 2 - 4 * lax.div(t, 2)
    greeted = (
        [(3, T - 1 - t), (2, col_dev), (1, row_dev)]
        if square
        else [(n, lax.rem(t + n, T)) for n in range(1, T)]
    )

    far_pairs = G // 2 - 1
    mine, beside = G - 1, G - 2

    def way(k):
        static = isinstance(k, int)
        if static and k >= beside:
            return mine - k
        pair = k // 2 if static else lax.div(k, 2)
        odd = k % 2 if static else lax.rem(k, 2)
        return 2 * (far_pairs - pair) + odd

    def at_way(mask):
        if not paired:
            return lax.rem(g + mask, G)
        out, bit = 0, 1
        while bit < G:
            a = lax.rem(lax.div(g, bit), 2)
            b = mask // bit % 2 if isinstance(mask, int) else lax.rem(lax.div(mask, bit), 2)
            out = out + bit * (a + b - 2 * a * b)
            bit *= 2
        return out

    def peer_g(k):
        return at_way(way(k))

    def from_g(k):
        return peer_g(k) if paired else at_way(G - way(k))

    level = lax.div(g, 2)
    first = far_pairs - lax.max(level, 1)

    def turn(i):
        if not paired:
            return i
        later = i - 1 + jnp.where(i > first, 1, 0)
        return jnp.where(i == 0, first, later)

    def turn_in(i):
        return jnp.where(first == far_pairs - 1, i, turn(i)) if paired else i

    def over_t(src, dst, ssem, rsem, dev):
        return pltpu.make_async_remote_copy(
            src_ref=src, dst_ref=dst, send_sem=ssem, recv_sem=rsem,
            device_id=(g, dev), device_id_type=MESH,
        )

    def over_g(src, dst, ssem, rsem, dev):
        return pltpu.make_async_remote_copy(
            src_ref=src, dst_ref=dst, send_sem=ssem, recv_sem=rsem,
            device_id=(dev, t), device_id_type=MESH,
        )

    def c_zq(k):
        return over_g(zq.at[k], qall.at[t, RES_DEV + k], zq_s.at[0], zq_r.at[k], peer_g(k))

    near = greeted[1:] if square else greeted

    def send_own(s, devs):
        own = qall.at[t, s]
        for _, dev in devs:
            over_t(own, own, q_s.at[0], q_r.at[s], dev).start()

    def whole(s):
        rest = qall.at[pl.ds(0, T - 1), s]
        over_t(rest, rest, q_s.at[0], q_r.at[s], t).wait_recv()

    def c_o(b, j, n, p):
        rows = pl.ds(pl.multiple_of(j * R, R), R)
        return over_t(
            obuf.at[b, p, :, rows], rbuf.at[b, back(n), :, rows], o_s.at[0], o_r.at[b], p
        )

    def c_st(b, n, p):
        return over_t(sbuf.at[b, p], rstat.at[b, back(n)], st_s.at[0], st_r.at[b], p)

    def back(n):
        return n if square else T - n

    barrier = pltpu.get_barrier_semaphore()
    moving = [k for k in range(G) if k != mine]

    def when_above(k, act):
        @pl.when(peer_g(k) > g)
        def _():
            act()

    def when_below(k, act):
        @pl.when(peer_g(k) < g)
        def _():
            act()

    def greet(k):
        pl.semaphore_signal(barrier, inc=1, device_id=(peer_g(k), t), device_id_type=MESH)

    def answer(k):
        back = k if paired else [way(m) for m in range(G)].index((G - way(k)) % G)
        pl.semaphore_signal(
            above.at[back // 2 if paired else back], inc=1, device_id=(peer_g(k), t), device_id_type=MESH
        )

    def late(k):
        @pl.when(peer_g(k) > g)
        def _():
            if not paired:
                pl.semaphore_wait(above.at[k], 1)
            elif k % 2 == 0:
                pl.semaphore_wait(above.at[k // 2], 1 if k == beside else 2)
            c_zq(k).start()

    def meet():
        pl.semaphore_wait(barrier, g + len(near))
        for k in moving:
            when_below(k, functools.partial(answer, k))
        if square:
            pl.semaphore_signal(
                across.at[0], inc=1, device_id=(g, row_dev), device_id_type=MESH
            )

    for k in moving:
        when_above(k, functools.partial(greet, k))
    for _, dev in near:
        pl.semaphore_signal(barrier, inc=1, device_id=(g, dev), device_id_type=MESH)
    load_q = pltpu.make_async_copy(q_hbm, q_in, load_sem.at[2])
    load_new = pltpu.make_async_copy(new_hbm, new_in, load_sem.at[3])
    load_pre = pltpu.make_async_copy(pre_hbm, cache.at[0:MIG_DEV], load_sem.at[4])
    load_res = pltpu.make_async_copy(res_hbm, cache.at[MIG_DEV:PER_GROUP], load_sem.at[4])
    tables = [
        pltpu.make_async_copy(src, dst, load_sem.at[i // 3])
        for i, (src, dst) in enumerate(
            (
                (kept_hbm, plan_v.at[0:1]),
                (home_hbm, plan_v.at[1:2]),
                (dest_hbm, plan_v.at[2:3]),
                (stay_hbm, kept),
            )
        )
    ]
    for copy in tables:
        copy.start()
    load_q.start()
    load_new.start()
    meet()
    load_q.wait()

    def arrange(row):
        for h in range(HB):
            piece = q_in[row, :, h * HD : (h + 1) * HD]
            stage[row, h * STEPS : (h + 1) * STEPS, :] = piece.astype(F32)

    for j in range(RES_DEV):
        arrange(j)
        qall[t, j] = stage[j].astype(BF16)
    for j in range(RES_DEV):
        send_own(j, near)
    for row in range(RES_DEV, PER_GROUP):
        arrange(row)
    pltpu.make_async_copy(plan_v, plan_v, load_sem.at[0]).wait()
    tables[3].wait()
    load_pre.start()
    load_res.start()
    sources = [from_g(k) for k in range(G)]
    fill_table([peer_g(k) for k in range(G)], sources, g, plan_v, tab_v)
    load_tab = pltpu.make_async_copy(tab_v, tab_s, load_sem.at[2])
    load_tab.start()
    load_tab.wait()

    for k in range(G):
        block = stage[tab_s[k, 0]].astype(BF16)
        zq[k] = block
        if k == mine:
            qall[t, RES_DEV + k] = block

    for k in reversed(moving):
        when_below(k, c_zq(k).start)
    send_own(RES_DEV + mine, near)

    kv_col = pl.multiple_of((t * KVL * KVH) // (T * KVL) * HD, HD)

    def stage_new(b):
        for j in range(BATCH):
            row = b * BATCH + j if b < STAY else tab_s[(b - STAY) * BATCH + j, 0]
            for c in range(2):
                for i in range(KVL):
                    lo = (i * BATCH + j) * STEPS
                    col = pl.multiple_of(c * half + kv_col + i * HD, HD)
                    newk[b, c, lo : lo + STEPS, :] = new_in[row, :, pl.ds(col, HD)].astype(F32)

    def asked_of(b, j):
        return qall[t, b * BATCH + j] if b < STAY else zq[(b - STAY) * BATCH + j]

    r16 = lax.broadcasted_iota(jnp.int32, (KVL * BATCH * STEPS, PW), 0)
    lanes16 = lax.broadcasted_iota(jnp.int32, (KVL * BATCH * STEPS, PW), 1)
    causal = (r16 // STEPS == lanes16 // R) & (r16 % STEPS <= lanes16 % STEPS)

    def new_here(_):
        load_new.wait()

    def fresh(b):
        stage_new(b)
        asked = jnp.concatenate(
            [asked_of(b, j)[i * R : (i + 1) * R] for i in range(KVL) for j in range(BATCH)],
            axis=0,
        )
        keys, values = newk[b, 0].astype(BF16), newk[b, 1].astype(BF16)
        scores = lax.dot_general(keys, asked, NT, preferred_element_type=F32) * SCALE
        scores = jnp.where(causal, scores, NEG_FLOOR)
        top = jnp.max(scores, axis=0, keepdims=True)
        weights = jnp.where(causal, jnp.exp(scores - top), 0.0)
        nstat[b, 0:1, :] = top
        nstat[b, 1:2, :] = jnp.sum(weights, axis=0, keepdims=True)
        nadd[b] = lax.dot_general(
            weights.astype(BF16), values, TN, preferred_element_type=F32
        )

    def forward(k):
        came = qall.at[t, RES_DEV + k]
        over_g(came, came, zq_s.at[0], zq_r.at[k], g).wait_recv()
        send_own(RES_DEV + k, greeted)

    def attend_slot(row, length, slot, b, j, hold=False):
        lane = lax.broadcasted_iota(jnp.int32, (R, 128), 1)
        usable = offset + lax.broadcasted_iota(jnp.int32, (R, pos), 1) < length
        stats = [jnp.zeros((R, 128), F32) for _ in range(KVL)]
        rows = pl.ds(pl.multiple_of(j * R, R), R)
        W = 2 if KVL % 2 == 0 else 1
        units = [(tt, i) for tt in range(T) for i in range(0, KVL, W)]
        all_scores = []
        for tt, i in units:
            kv = (tt * KVL + i) * KVH // (T * KVL)
            asked = qall[tt, slot, i * R : (i + W) * R, :]
            keys = jnp.concatenate(
                [cache[row, :, (kv + w) * HD : (kv + w + 1) * HD] for w in range(W)], axis=0
            )
            scores = lax.dot_general(asked, keys, NT, preferred_element_type=F32)
            all_scores.append(
                [scores[w * R : (w + 1) * R, w * pos : (w + 1) * pos] * SCALE for w in range(W)]
            )
        all_weights = []
        for (tt, i), scores in zip(units, all_scores):
            rounded = []
            for w in range(W):
                masked = jnp.where(usable, scores[w], NEG_FLOOR)
                highest = jnp.max(masked, axis=1, keepdims=True)
                weights = jnp.where(usable, jnp.exp(masked - highest), 0.0)
                total = jnp.sum(weights, axis=1, keepdims=True)
                rounded.append(weights.astype(BF16))
                stats[i + w] = jnp.where(lane == 2 * tt, highest, stats[i + w])
                stats[i + w] = jnp.where(lane == 2 * tt + 1, total, stats[i + w])
            all_weights.append(jnp.concatenate(rounded, axis=0))
        for (tt, i), weights in zip(units, all_weights):
            kv = (tt * KVL + i) * KVH // (T * KVL)
            values = cache[row, :, half + kv * HD : half + (kv + W) * HD]
            blended = jnp.dot(weights, values, preferred_element_type=F32)
            for w in range(W):
                obuf[b, tt, i + w, rows, :] = blended[
                    w * R : (w + 1) * R, w * HD : (w + 1) * HD
                ].astype(BF16)
        for i in range(KVL):
            statbuf[pl.ds(pl.multiple_of(i * LW + j * R, R), R), :] = stats[i]
        if not hold:
            for n, p in greeted:
                c_o(b, j, n, p).start()

    def send_stats(b):
        for n, p in greeted:
            c_st(b, n, p).start()
        rbuf[b, 0] = obuf[b, t]
        rstat[b, 0] = sbuf[b, t]

    rest = pl.ds(1, T - 1)

    def loaded(_):
        pltpu.make_async_copy(cache, cache, load_sem.at[4]).wait()

    def turn_stats(b):
        turned = statbuf[...].T
        for tt in range(T):
            sbuf[b, tt] = turned[2 * tt : 2 * tt + 2, :]

    def stay_batch(b, hold=True):
        @pl.loop(0, BATCH)
        def _(j):
            s = b * BATCH + j
            whole(s)
            attend_slot(MIG_DEV + s, kept[0, g * RES_DEV + s], s, b, j, hold)

        turn_stats(b)
        if not hold:
            send_stats(b)

    def moved_batch(b, hold=False):
        @pl.loop(0, BATCH)
        def _(j):
            k = (b - STAY) * BATCH + j
            whole(RES_DEV + k)
            held = tab_s[G + k, 0]
            attend_slot(held % MIG_DEV, held // MIG_DEV, RES_DEV + k, b, j, hold)

        turn_stats(b)
        if not hold:
            send_stats(b)

    def send_batch(b):
        for j in range(BATCH):
            for n, p in greeted:
                c_o(b, j, n, p).start()
        send_stats(b)

    def reach(_):
        if square:
            pl.semaphore_wait(across.at[0], 1)
            for s in (*range(RES_DEV), RES_DEV + mine):
                send_own(s, greeted[:1])

    def stays():
        pl.loop(0, STAY)(stay_batch)

    def locals_held(_):
        moved_batch(NB - 1, True)

    def far(_):
        @pl.loop(0, far_pairs)
        def _(i):
            moved_batch(STAY + turn(i))

    def forward_pair(i):
        for j in range(2):
            forward(2 * turn_in(i) + j)

    def forward_rest(_):
        pl.loop(1, far_pairs - 1)(forward_pair)


    F, N, L = forward, fresh, late
    middle = list(range(2, beside))
    early = g < G // 4

    def stays_early(_):
        @pl.when(early)
        def _():
            stay_batch(0, False)
            pl.loop(1, STAY)(stay_batch)

    def first_stay_late(_):
        @pl.when(jnp.logical_not(early))
        def _():
            stay_batch(0)

    def stays_late(_):
        @pl.when(jnp.logical_not(early))
        def _():
            pl.loop(1, STAY)(stay_batch)

    def held_late(_):
        pl.when(jnp.logical_not(early))(functools.partial(send_batch, 0))
        for b in range(1, STAY):
            send_batch(b)

    plan = [(reach, 0), (L, beside), (new_here, 0), (N, 0), (L, beside - 2), (L, beside - 1), (F, beside)]
    plan += [(N, 1)] + [(L, k + j) for k in reversed(range(0, beside - 2, 2)) for j in range(2)] + [(N, NB - 1)]
    plan += [(F, beside - 2), (F, beside - 1), (loaded, 0), (stays_early, 0)]
    plan += [(forward_pair, 0), (first_stay_late, 0), (forward_rest, 0)]
    plan += [(stays_late, 0), (locals_held, 0), (far, 0), (send_batch, NB - 1)]
    plan += [(held_late, 0)]
    plan += [(N, b) for b in range(STAY, NB - 1)]
    for step, p in plan:
        step(p)

    def arrived(b):
        over_t(rstat.at[b, rest], rstat.at[b, rest], st_s.at[0], st_r.at[b], t).wait_recv()
        over_t(rbuf.at[b, rest], rbuf.at[b, rest], o_s.at[0], o_r.at[b], t).wait_recv()

    def factors_of(b):
        tops = [rstat[b, n][0:1] for n in range(T)]
        highest = functools.reduce(jnp.maximum, tops)
        factors = [jnp.exp(top - highest) for top in tops]
        total = factors[0] * rstat[b, 0][1:2]
        for n in range(1, T):
            total = total + factors[n] * rstat[b, n][1:2]
        return highest, total, factors

    def columns_of(place, rows):
        for i, row in enumerate(rows):
            facbuf[place, i : i + 1, :] = row
        return facbuf[place].T

    def blend(b, columns):
        blended = rbuf[b, 0].reshape(PW, HD).astype(F32) * columns[:, 0:1]
        for n in range(1, T):
            blended = blended + rbuf[b, n].reshape(PW, HD).astype(F32) * columns[:, n : n + 1]
        return blended

    def merged(b):
        highest, total, factors = factors_of(b)
        return highest, total, blend(b, columns_of(b, factors))

    def with_new(b, highest, total):
        top = jnp.maximum(highest, nstat[b, 0:1])
        old_part, new_part = jnp.exp(highest - top), jnp.exp(nstat[b, 0:1] - top)
        inverse = 1.0 / (total * old_part + nstat[b, 1:2] * new_part)
        return old_part * inverse, new_part * inverse

    def keep(b, done):
        for j in range(BATCH):
            for i in range(KVL):
                lo = i * LW + j * R
                fin[b * BATCH + j, i * R : (i + 1) * R, :] = done[lo : lo + R]

    def finish(b, highest, total, blended):
        columns = columns_of(NB + b, with_new(b, highest, total))
        keep(b, blended * columns[:, 0:1] + nadd[b] * columns[:, 1:2])

    def put(slot, row):
        for h in range(HB):
            piece = fin[slot, h * STEPS : (h + 1) * STEPS, :]
            out[row, :, h * HD : (h + 1) * HD] = piece.astype(BF16)

    def give_back(b):
        arrived(b)
        highest, total, blended = merged(b)
        zs[b - STAY] = jnp.concatenate([highest, total], axis=0)
        for j in range(BATCH):
            k = (b - STAY) * BATCH + j
            for i in range(KVL):
                zo[k, i] = blended[i * LW + j * R : i * LW + (j + 1) * R].astype(BF16)
            if isinstance(k, int) and k == mine:
                zrs[k] = zs[b - STAY]
                zro[k] = zo[k]
            else:
                pair, dev = b - STAY, from_g(k)
                over_g(zs.at[pair], zrs.at[k], zs_s.at[0], zs_r.at[pair], dev).start()
                over_g(zo.at[k], zro.at[k], zo_s.at[0], zo_r.at[pair], dev).start()

    def give_far(_):
        @pl.loop(0, far_pairs)
        def _(i):
            give_back(STAY + turn(i))

    def end_stay(b):
        highest, total, factors = factors_of(b)
        old, new = with_new(b, highest, total)
        columns = columns_of(b, [factor * old for factor in factors] + [new])
        keep(b, blend(b, columns) + nadd[b] * columns[:, T : T + 1])

    def returned(b):
        first = (b - STAY) * BATCH
        came = pl.ds(first, BATCH - (first <= mine < first + BATCH))
        over_g(zrs.at[came], zrs.at[came], zs_s.at[0], zs_r.at[b - STAY], g).wait_recv()
        over_g(zro.at[came], zro.at[came], zo_s.at[0], zo_r.at[b - STAY], g).wait_recv()

    def end_moved(b):
        lanes = lax.broadcasted_iota(jnp.int32, (2, PW), 1)
        stats = jnp.zeros((2, PW), F32)
        first = (b - STAY) * BATCH
        for j in range(BATCH):
            stats = jnp.where((lanes // R) % BATCH == j, zrs[first + j], stats)
        blended = jnp.concatenate(
            [zro[first + j, i].astype(F32) for i in range(KVL) for j in range(BATCH)], axis=0
        )
        finish(b, stats[0:1], stats[1:2], blended)

    moved = list(range(STAY, NB))
    def stay_early(_):
        @pl.when(early)
        def _():
            arrived(0)
            end_stay(0)

    def stay_late(_):
        @pl.when(jnp.logical_not(early))
        def _():
            arrived(0)
            end_stay(0)

    plan = [(stay_early, 0), (give_far, 0), (give_back, moved[-1]), (stay_late, 0)]
    last = [moved[0], moved[-1]]
    plan += [(returned, b) for b in moved[1:-1]] + [(end_moved, b) for b in moved[1:-1]]
    plan += [(returned, b) for b in last] + [(arrived, b) for b in range(1, STAY)]
    plan += [(end_moved, b) for b in last] + [(end_stay, b) for b in range(1, STAY)]
    for step, p in plan:
        step(p)
    for j in range(RES_DEV):
        put(j, j)
    for l in range(MIG_DEV):
        k_of = 0
        for k in range(G):
            k_of = jnp.where(tab_s[k, 0] == RES_DEV + l, k, k_of)
        put(RES_DEV + k_of, RES_DEV + l)

    others = pl.ds(1, G - 1)
    over_g(zq.at[others], zq.at[others], zq_s.at[0], zq_r.at[0], g).wait_send()
    over_g(zrs.at[others], zrs.at[others], zs_s.at[0], zs_r.at[0], g).wait_send()
    over_g(zo.at[others], zo.at[others], zo_s.at[0], zo_r.at[0], g).wait_send()
    sent = qall.at[pl.ds(0, T - 1)]
    over_t(sent, sent, q_s.at[0], q_r.at[0], t).wait_send()
    stats, parts = rstat.at[:, rest], rbuf.at[:, rest]
    over_t(stats, stats, st_s.at[0], st_r.at[0], t).wait_send()
    over_t(parts, parts, o_s.at[0], o_r.at[0], t).wait_send()


def body(
    queries,
    new_entries,
    resident_cache,
    prefill_cache,
    resident_kept,
    kept_tokens,
    prefill_slot,
    decode_slot,
):
    G = lax.axis_size("group")
    T = lax.axis_size("tensor")
    KVL = max(1, KVH // T)
    HB = H // T
    RB = STEPS * HB
    R = RB // KVL
    LW = BATCH * R
    NB = STAY + G // BATCH
    PW = KVL * LW
    dma = pltpu.SemaphoreType.DMA
    vmem = pl.BlockSpec(memory_space=pltpu.VMEM)
    hbm = pl.BlockSpec(memory_space=pl.ANY)
    return pl.pallas_call(
        functools.partial(kernel, G, T),
        out_shape=pltpu.VMEM(queries.shape, BF16),
        in_specs=[hbm] * 8,
        out_specs=vmem,
        scratch_shapes=[
            pltpu.VMEM((3, kept_tokens.shape[0]), jnp.int32),
            pltpu.SMEM((1, resident_kept.shape[0]), jnp.int32),
            pltpu.VMEM((2 * G, 128), jnp.int32),
            pltpu.SMEM((2 * G, 128), jnp.int32),
            pltpu.VMEM(queries.shape, BF16),
            pltpu.VMEM(new_entries.shape, BF16),
            pltpu.VMEM((PER_GROUP, *resident_cache.shape[1:]), BF16),
            pltpu.VMEM((T, RES_DEV + G, RB, HD), BF16),
            pltpu.VMEM((G, RB, HD), BF16),
            pltpu.VMEM((PER_GROUP, RB, HD), F32),
            pltpu.VMEM((NB, T, KVL, LW, HD), BF16),
            pltpu.VMEM((NB, T, KVL, LW, HD), BF16),
            pltpu.VMEM((NB, T, 2, PW), F32),
            pltpu.VMEM((NB, T, 2, PW), F32),
            pltpu.VMEM((PW, 128), F32),
            pltpu.VMEM((2 * NB, -(-(T + 1) // 8) * 8, PW), F32),
            pltpu.VMEM((G, KVL, R, HD), BF16),
            pltpu.VMEM((G, KVL, R, HD), BF16),
            pltpu.VMEM((NB - STAY, 2, PW), F32),
            pltpu.VMEM((G, 2, PW), F32),
            pltpu.VMEM((NB, 2, KVL * BATCH * STEPS, HD), F32),
            pltpu.VMEM((NB, 2, PW), F32),
            pltpu.VMEM((NB, PW, HD), F32),
            pltpu.VMEM((NB * BATCH, RB, HD), F32),
            dma((5,)),
            pltpu.SemaphoreType.REGULAR((G // 2 if G & (G - 1) == 0 else G,)),
            pltpu.SemaphoreType.REGULAR((1,)),
            dma((1,)),
            dma((G,)),
            dma((1,)),
            dma((RES_DEV + G,)),
            dma((1,)),
            dma((NB,)),
            dma((1,)),
            dma((NB,)),
            dma((1,)),
            dma((NB - STAY,)),
            dma((1,)),
            dma((NB - STAY,)),
        ],
        compiler_params=pltpu.CompilerParams(collective_id=0, has_side_effects=True),
    )(
        kept_tokens[None],
        prefill_slot[None],
        decode_slot[None],
        resident_kept[None],
        queries, new_entries, resident_cache, prefill_cache)


def solution(mesh):
    in_specs = (
        P("group", None, "tensor"),
        P("group", None, None),
        P("group", "tensor", None),
        P("group", "tensor", None),
        P(),
        P(),
        P(),
        P(),
    )
    out_specs = P("group", None, "tensor")
    return jax.shard_map(body, mesh=mesh, in_specs=in_specs, out_specs=out_specs, check_vma=False)
```

```python
import functools
import math

import jax
import jax.numpy as jnp
from jax import lax
from jax.experimental import pallas as pl
from jax.experimental.pallas import tpu as pltpu
from jax.sharding import PartitionSpec as P

H = 64
KVH = 8
HD = 128
STEPS = 4
MIG_DEV = 8
RES_DEV = 4
PER_GROUP = RES_DEV + MIG_DEV
BATCH = 2
STAY = RES_DEV // BATCH

NEG_FLOOR = -1e30
SCALE = 1.0 / math.sqrt(HD)
MESH = pl.DeviceIdType.MESH
F32 = jnp.float32
BF16 = jnp.bfloat16
NT = (((1,), (1,)), ((), ()))
TN = (((0,), (0,)), ((), ()))


def flipped(v, mask):
    out, bit = v, 1
    while bit <= mask:
        if mask & bit:
            out = out + bit * (1 - 2 * lax.rem(lax.div(v, bit), 2))
        bit *= 2
    return out


def fill_table(peers, sources, g, plan_v, tab_v):
    G = len(peers)
    shape = (2 * G, plan_v.shape[1])
    n = lax.broadcasted_iota(jnp.int32, shape, 0)
    dest = jnp.broadcast_to(plan_v[2:3, :], shape)
    home = jnp.broadcast_to(plan_v[1:2, :], shape)
    kept = jnp.broadcast_to(plan_v[0:1, :], shape)
    dest_group, home_group = lax.div(dest, PER_GROUP), lax.div(home, MIG_DEV)
    other = jnp.zeros(shape, jnp.int32)
    for k in range(G):
        other = jnp.where(n == k, peers[k], other)
        other = jnp.where(n == G + k, sources[k], other)
    arriving = (n < G) & (dest_group == g) & (home_group == other)
    leaving = (n >= G) & (home_group == g) & (dest_group == other)
    picked = jnp.where(arriving, dest - dest_group * PER_GROUP, 0)
    held = home - home_group * MIG_DEV + MIG_DEV * kept
    picked = picked + jnp.where(leaving, held, 0)
    total = jnp.sum(picked, axis=1, keepdims=True)
    tab_v[...] = jnp.broadcast_to(total, tab_v.shape)


def kernel(
    G,
    T,
    kept_hbm,
    home_hbm,
    dest_hbm,
    stay_hbm,
    q_hbm,
    new_hbm,
    res_hbm,
    pre_hbm,
    out,
    plan_v,
    kept,
    tab_v,
    tab_s,
    q_in,
    new_in,
    cache,
    qall,
    zq,
    stage,
    obuf,
    rbuf,
    sbuf,
    rstat,
    statbuf,
    facbuf,
    zo,
    zro,
    zs,
    zrs,
    newk,
    nstat,
    nadd,
    fin,
    load_sem,
    above,
    across,
    zq_s,
    zq_r,
    q_s,
    q_r,
    o_s,
    o_r,
    st_s,
    st_r,
    zo_s,
    zo_r,
    zs_s,
    zs_r,
):
    KVL = max(1, KVH // T)
    HB = H // T
    HU = HB // KVL
    R = STEPS * HU
    LW = BATCH * R
    PW = KVL * LW
    NB = STAY + G // BATCH
    pos = cache.shape[1]
    half = KVH * HD
    g = lax.axis_index("group")
    t = lax.axis_index("tensor")
    offset = t * pos

    paired = G & (G - 1) == 0
    square = T == 4
    row_dev = t + 1 - 2 * lax.rem(t, 2)
    col_dev = t + 2 - 4 * lax.div(t, 2)
    greeted = (
        [(3, T - 1 - t), (2, col_dev), (1, row_dev)]
        if square
        else [(n, lax.rem(t + n, T)) for n in range(1, T)]
    )

    far_pairs = G // 2 - 1
    mine, beside = G - 1, G - 2

    def way(k):
        static = isinstance(k, int)
        if static and k >= beside:
            return mine - k
        pair = k // 2 if static else lax.div(k, 2)
        odd = k % 2 if static else lax.rem(k, 2)
        return 2 * (far_pairs - pair) + odd

    def at_way(mask):
        if not paired:
            return lax.rem(g + mask, G)
        out, bit = 0, 1
        while bit < G:
            a = lax.rem(lax.div(g, bit), 2)
            b = mask // bit % 2 if isinstance(mask, int) else lax.rem(lax.div(mask, bit), 2)
            out = out + bit * (a + b - 2 * a * b)
            bit *= 2
        return out

    def peer_g(k):
        return at_way(way(k))

    def from_g(k):
        return peer_g(k) if paired else at_way(G - way(k))

    level = lax.div(g, 2)
    first = far_pairs - lax.max(level, 1)

    def turn(i):
        if not paired:
            return i
        later = i - 1 + jnp.where(i > first, 1, 0)
        return jnp.where(i == 0, first, later)

    def turn_in(i):
        return jnp.where(first == far_pairs - 1, i, turn(i)) if paired else i

    def over_t(src, dst, ssem, rsem, dev):
        return pltpu.make_async_remote_copy(
            src_ref=src, dst_ref=dst, send_sem=ssem, recv_sem=rsem,
            device_id=(g, dev), device_id_type=MESH,
        )

    def over_g(src, dst, ssem, rsem, dev):
        return pltpu.make_async_remote_copy(
            src_ref=src, dst_ref=dst, send_sem=ssem, recv_sem=rsem,
            device_id=(dev, t), device_id_type=MESH,
        )

    def c_zq(k):
        return over_g(zq.at[k], qall.at[t, RES_DEV + k], zq_s.at[0], zq_r.at[k], peer_g(k))

    near = greeted[1:] if square else greeted

    def send_own(s, devs):
        own = qall.at[t, s]
        for _, dev in devs:
            over_t(own, own, q_s.at[0], q_r.at[s], dev).start()

    def whole(s):
        rest = qall.at[pl.ds(0, T - 1), s]
        over_t(rest, rest, q_s.at[0], q_r.at[s], t).wait_recv()

    def c_o(b, j, n, p):
        rows = pl.ds(pl.multiple_of(j * R, R), R)
        return over_t(
            obuf.at[b, p, :, rows], rbuf.at[b, back(n), :, rows], o_s.at[0], o_r.at[b], p
        )

    def c_st(b, n, p):
        return over_t(sbuf.at[b, p], rstat.at[b, back(n)], st_s.at[0], st_r.at[b], p)

    def back(n):
        return n if square else T - n

    barrier = pltpu.get_barrier_semaphore()
    moving = [k for k in range(G) if k != mine]

    def when_above(k, act):
        @pl.when(peer_g(k) > g)
        def _():
            act()

    def when_below(k, act):
        @pl.when(peer_g(k) < g)
        def _():
            act()

    def greet(k):
        pl.semaphore_signal(barrier, inc=1, device_id=(peer_g(k), t), device_id_type=MESH)

    def answer(k):
        back = k if paired else [way(m) for m in range(G)].index((G - way(k)) % G)
        pl.semaphore_signal(
            above.at[back // 2 if paired else back], inc=1, device_id=(peer_g(k), t), device_id_type=MESH
        )

    def late(k):
        @pl.when(peer_g(k) > g)
        def _():
            if not paired:
                pl.semaphore_wait(above.at[k], 1)
            elif k % 2 == 0:
                pl.semaphore_wait(above.at[k // 2], 1 if k == beside else 2)
            c_zq(k).start()

    def meet():
        pl.semaphore_wait(barrier, g + len(near))
        for k in moving:
            when_below(k, functools.partial(answer, k))
        if square:
            pl.semaphore_signal(
                across.at[0], inc=1, device_id=(g, row_dev), device_id_type=MESH
            )

    for k in moving:
        when_above(k, functools.partial(greet, k))
    for _, dev in near:
        pl.semaphore_signal(barrier, inc=1, device_id=(g, dev), device_id_type=MESH)
    load_q = pltpu.make_async_copy(q_hbm, q_in, load_sem.at[2])
    load_new = pltpu.make_async_copy(new_hbm, new_in, load_sem.at[3])
    load_pre = pltpu.make_async_copy(pre_hbm, cache.at[0:MIG_DEV], load_sem.at[4])
    load_res = pltpu.make_async_copy(res_hbm, cache.at[MIG_DEV:PER_GROUP], load_sem.at[4])
    tables = [
        pltpu.make_async_copy(src, dst, load_sem.at[i // 3])
        for i, (src, dst) in enumerate(
            (
                (kept_hbm, plan_v.at[0:1]),
                (home_hbm, plan_v.at[1:2]),
                (dest_hbm, plan_v.at[2:3]),
                (stay_hbm, kept),
            )
        )
    ]
    for copy in tables:
        copy.start()
    load_q.start()
    load_new.start()
    meet()
    load_q.wait()

    def arrange(row):
        for h in range(HB):
            piece = q_in[row, :, h * HD : (h + 1) * HD]
            stage[row, h * STEPS : (h + 1) * STEPS, :] = piece.astype(F32)

    for j in range(RES_DEV):
        arrange(j)
        qall[t, j] = stage[j].astype(BF16)
    for j in range(RES_DEV):
        send_own(j, near)
    for row in range(RES_DEV, PER_GROUP):
        arrange(row)
    pltpu.make_async_copy(plan_v, plan_v, load_sem.at[0]).wait()
    tables[3].wait()
    load_pre.start()
    load_res.start()
    sources = [from_g(k) for k in range(G)]
    fill_table([peer_g(k) for k in range(G)], sources, g, plan_v, tab_v)
    load_tab = pltpu.make_async_copy(tab_v, tab_s, load_sem.at[2])
    load_tab.start()
    load_tab.wait()

    for k in range(G):
        block = stage[tab_s[k, 0]].astype(BF16)
        zq[k] = block
        if k == mine:
            qall[t, RES_DEV + k] = block

    for k in reversed(moving):
        when_below(k, c_zq(k).start)
    send_own(RES_DEV + mine, near)

    kv_col = pl.multiple_of((t * KVL * KVH) // (T * KVL) * HD, HD)

    def stage_new(b):
        for j in range(BATCH):
            row = b * BATCH + j if b < STAY else tab_s[(b - STAY) * BATCH + j, 0]
            for c in range(2):
                for i in range(KVL):
                    lo = (i * BATCH + j) * STEPS
                    col = pl.multiple_of(c * half + kv_col + i * HD, HD)
                    newk[b, c, lo : lo + STEPS, :] = new_in[row, :, pl.ds(col, HD)].astype(F32)

    def asked_of(b, j):
        return qall[t, b * BATCH + j] if b < STAY else zq[(b - STAY) * BATCH + j]

    r16 = lax.broadcasted_iota(jnp.int32, (KVL * BATCH * STEPS, PW), 0)
    lanes16 = lax.broadcasted_iota(jnp.int32, (KVL * BATCH * STEPS, PW), 1)
    causal = (r16 // STEPS == lanes16 // R) & (r16 % STEPS <= lanes16 % STEPS)

    def new_here(_):
        load_new.wait()

    def fresh(b):
        stage_new(b)
        asked = jnp.concatenate(
            [asked_of(b, j)[i * R : (i + 1) * R] for i in range(KVL) for j in range(BATCH)],
            axis=0,
        )
        keys, values = newk[b, 0].astype(BF16), newk[b, 1].astype(BF16)
        scores = lax.dot_general(keys, asked, NT, preferred_element_type=F32) * SCALE
        scores = jnp.where(causal, scores, NEG_FLOOR)
        top = jnp.max(scores, axis=0, keepdims=True)
        weights = jnp.where(causal, jnp.exp(scores - top), 0.0)
        nstat[b, 0:1, :] = top
        nstat[b, 1:2, :] = jnp.sum(weights, axis=0, keepdims=True)
        nadd[b] = lax.dot_general(
            weights.astype(BF16), values, TN, preferred_element_type=F32
        )

    def forward(k):
        came = qall.at[t, RES_DEV + k]
        over_g(came, came, zq_s.at[0], zq_r.at[k], g).wait_recv()
        send_own(RES_DEV + k, greeted)

    def attend_slot(row, length, slot, b, j, hold=False):
        lane = lax.broadcasted_iota(jnp.int32, (R, 128), 1)
        usable = offset + lax.broadcasted_iota(jnp.int32, (R, pos), 1) < length
        stats = [jnp.zeros((R, 128), F32) for _ in range(KVL)]
        rows = pl.ds(pl.multiple_of(j * R, R), R)
        W = 2 if KVL % 2 == 0 else 1
        units = [(tt, i) for tt in range(T) for i in range(0, KVL, W)]
        all_scores = []
        for tt, i in units:
            kv = (tt * KVL + i) * KVH // (T * KVL)
            asked = qall[tt, slot, i * R : (i + W) * R, :]
            keys = jnp.concatenate(
                [cache[row, :, (kv + w) * HD : (kv + w + 1) * HD] for w in range(W)], axis=0
            )
            scores = lax.dot_general(asked, keys, NT, preferred_element_type=F32)
            all_scores.append(
                [scores[w * R : (w + 1) * R, w * pos : (w + 1) * pos] * SCALE for w in range(W)]
            )
        all_weights = []
        for (tt, i), scores in zip(units, all_scores):
            rounded = []
            for w in range(W):
                masked = jnp.where(usable, scores[w], NEG_FLOOR)
                highest = jnp.max(masked, axis=1, keepdims=True)
                weights = jnp.where(usable, jnp.exp(masked - highest), 0.0)
                total = jnp.sum(weights, axis=1, keepdims=True)
                rounded.append(weights.astype(BF16))
                stats[i + w] = jnp.where(lane == 2 * tt, highest, stats[i + w])
                stats[i + w] = jnp.where(lane == 2 * tt + 1, total, stats[i + w])
            all_weights.append(jnp.concatenate(rounded, axis=0))
        for (tt, i), weights in zip(units, all_weights):
            kv = (tt * KVL + i) * KVH // (T * KVL)
            values = cache[row, :, half + kv * HD : half + (kv + W) * HD]
            blended = jnp.dot(weights, values, preferred_element_type=F32)
            for w in range(W):
                obuf[b, tt, i + w, rows, :] = blended[
                    w * R : (w + 1) * R, w * HD : (w + 1) * HD
                ].astype(BF16)
        for i in range(KVL):
            statbuf[pl.ds(pl.multiple_of(i * LW + j * R, R), R), :] = stats[i]
        if not hold:
            for n, p in greeted:
                c_o(b, j, n, p).start()

    def send_stats(b):
        for n, p in greeted:
            c_st(b, n, p).start()
        rbuf[b, 0] = obuf[b, t]
        rstat[b, 0] = sbuf[b, t]

    rest = pl.ds(1, T - 1)

    def loaded(_):
        pltpu.make_async_copy(cache, cache, load_sem.at[4]).wait()

    def turn_stats(b):
        turned = statbuf[...].T
        for tt in range(T):
            sbuf[b, tt] = turned[2 * tt : 2 * tt + 2, :]

    def stay_batch(b, hold=True):
        @pl.loop(0, BATCH)
        def _(j):
            s = b * BATCH + j
            whole(s)
            attend_slot(MIG_DEV + s, kept[0, g * RES_DEV + s], s, b, j, hold)

        turn_stats(b)
        if not hold:
            send_stats(b)

    def moved_batch(b, hold=False):
        @pl.loop(0, BATCH)
        def _(j):
            k = (b - STAY) * BATCH + j
            whole(RES_DEV + k)
            held = tab_s[G + k, 0]
            attend_slot(held % MIG_DEV, held // MIG_DEV, RES_DEV + k, b, j, hold)

        turn_stats(b)
        if not hold:
            send_stats(b)

    def send_batch(b):
        for j in range(BATCH):
            for n, p in greeted:
                c_o(b, j, n, p).start()
        send_stats(b)

    def reach(_):
        if square:
            pl.semaphore_wait(across.at[0], 1)
            for s in (*range(RES_DEV), RES_DEV + mine):
                send_own(s, greeted[:1])

    def stays():
        pl.loop(0, STAY)(stay_batch)

    def locals_held(_):
        moved_batch(NB - 1, True)

    def far(_):
        @pl.loop(0, far_pairs)
        def _(i):
            moved_batch(STAY + turn(i))

    def forward_pair(i):
        for j in range(2):
            forward(2 * turn_in(i) + j)

    def forward_rest(_):
        pl.loop(1, far_pairs - 1)(forward_pair)


    F, N, L = forward, fresh, late
    middle = list(range(2, beside))
    early = g < G // 4

    def stays_early(_):
        @pl.when(early)
        def _():
            stay_batch(0, False)
            pl.loop(1, STAY)(stay_batch)

    def first_stay_late(_):
        @pl.when(jnp.logical_not(early))
        def _():
            stay_batch(0)

    def stays_late(_):
        @pl.when(jnp.logical_not(early))
        def _():
            pl.loop(1, STAY)(stay_batch)

    def held_late(_):
        pl.when(jnp.logical_not(early))(functools.partial(send_batch, 0))
        for b in range(1, STAY):
            send_batch(b)

    plan = [(new_here, 0), (N, 0), (reach, 0), (L, beside), (L, beside - 2), (L, beside - 1), (F, beside)]
    plan += [(N, 1)] + [(L, k + j) for k in reversed(range(0, beside - 2, 2)) for j in range(2)] + [(N, NB - 1)]
    plan += [(F, beside - 2), (F, beside - 1), (loaded, 0), (stays_early, 0)]
    plan += [(forward_pair, 0), (first_stay_late, 0), (forward_rest, 0)]
    plan += [(stays_late, 0), (locals_held, 0), (far, 0), (send_batch, NB - 1)]
    plan += [(held_late, 0)]
    plan += [(N, b) for b in range(STAY, NB - 1)]
    for step, p in plan:
        step(p)

    def arrived(b):
        over_t(rstat.at[b, rest], rstat.at[b, rest], st_s.at[0], st_r.at[b], t).wait_recv()
        over_t(rbuf.at[b, rest], rbuf.at[b, rest], o_s.at[0], o_r.at[b], t).wait_recv()

    def factors_of(b):
        tops = [rstat[b, n][0:1] for n in range(T)]
        highest = functools.reduce(jnp.maximum, tops)
        factors = [jnp.exp(top - highest) for top in tops]
        total = factors[0] * rstat[b, 0][1:2]
        for n in range(1, T):
            total = total + factors[n] * rstat[b, n][1:2]
        return highest, total, factors

    def columns_of(place, rows):
        for i, row in enumerate(rows):
            facbuf[place, i : i + 1, :] = row
        return facbuf[place].T

    def blend(b, columns):
        blended = rbuf[b, 0].reshape(PW, HD).astype(F32) * columns[:, 0:1]
        for n in range(1, T):
            blended = blended + rbuf[b, n].reshape(PW, HD).astype(F32) * columns[:, n : n + 1]
        return blended

    def merged(b):
        highest, total, factors = factors_of(b)
        return highest, total, blend(b, columns_of(b, factors))

    def with_new(b, highest, total):
        top = jnp.maximum(highest, nstat[b, 0:1])
        old_part, new_part = jnp.exp(highest - top), jnp.exp(nstat[b, 0:1] - top)
        inverse = 1.0 / (total * old_part + nstat[b, 1:2] * new_part)
        return old_part * inverse, new_part * inverse

    def keep(b, done):
        for j in range(BATCH):
            for i in range(KVL):
                lo = i * LW + j * R
                fin[b * BATCH + j, i * R : (i + 1) * R, :] = done[lo : lo + R]

    def finish(b, highest, total, blended):
        columns = columns_of(NB + b, with_new(b, highest, total))
        keep(b, blended * columns[:, 0:1] + nadd[b] * columns[:, 1:2])

    def put(slot, row):
        for h in range(HB):
            piece = fin[slot, h * STEPS : (h + 1) * STEPS, :]
            out[row, :, h * HD : (h + 1) * HD] = piece.astype(BF16)

    def give_back(b):
        arrived(b)
        highest, total, blended = merged(b)
        zs[b - STAY] = jnp.concatenate([highest, total], axis=0)
        for j in range(BATCH):
            k = (b - STAY) * BATCH + j
            for i in range(KVL):
                zo[k, i] = blended[i * LW + j * R : i * LW + (j + 1) * R].astype(BF16)
            if isinstance(k, int) and k == mine:
                zrs[k] = zs[b - STAY]
                zro[k] = zo[k]
            else:
                pair, dev = b - STAY, from_g(k)
                over_g(zs.at[pair], zrs.at[k], zs_s.at[0], zs_r.at[pair], dev).start()
                over_g(zo.at[k], zro.at[k], zo_s.at[0], zo_r.at[pair], dev).start()

    def give_far(_):
        @pl.loop(0, far_pairs)
        def _(i):
            give_back(STAY + turn(i))

    def end_stay(b):
        highest, total, factors = factors_of(b)
        old, new = with_new(b, highest, total)
        columns = columns_of(b, [factor * old for factor in factors] + [new])
        keep(b, blend(b, columns) + nadd[b] * columns[:, T : T + 1])

    def returned(b):
        first = (b - STAY) * BATCH
        came = pl.ds(first, BATCH - (first <= mine < first + BATCH))
        over_g(zrs.at[came], zrs.at[came], zs_s.at[0], zs_r.at[b - STAY], g).wait_recv()
        over_g(zro.at[came], zro.at[came], zo_s.at[0], zo_r.at[b - STAY], g).wait_recv()

    def end_moved(b):
        lanes = lax.broadcasted_iota(jnp.int32, (2, PW), 1)
        stats = jnp.zeros((2, PW), F32)
        first = (b - STAY) * BATCH
        for j in range(BATCH):
            stats = jnp.where((lanes // R) % BATCH == j, zrs[first + j], stats)
        blended = jnp.concatenate(
            [zro[first + j, i].astype(F32) for i in range(KVL) for j in range(BATCH)], axis=0
        )
        finish(b, stats[0:1], stats[1:2], blended)

    moved = list(range(STAY, NB))
    def stay_early(_):
        @pl.when(early)
        def _():
            arrived(0)
            end_stay(0)

    def stay_late(_):
        @pl.when(jnp.logical_not(early))
        def _():
            arrived(0)
            end_stay(0)

    plan = [(stay_early, 0), (give_far, 0), (give_back, moved[-1]), (stay_late, 0)]
    waits_long = early & (lax.rem(g, 2) == 1)

    def end_beside(_):
        returned(moved[-1])
        end_moved(moved[-1])

    def beside_soon(_):
        pl.when(jnp.logical_not(waits_long))(functools.partial(end_beside, 0))

    def beside_last(_):
        pl.when(waits_long)(functools.partial(end_beside, 0))

    plan += [(returned, b) for b in moved[1:-1]] + [(end_moved, b) for b in moved[1:-1]]
    plan += [(beside_soon, 0), (returned, moved[0])] + [(arrived, b) for b in range(1, STAY)]
    plan += [(end_moved, moved[0])] + [(end_stay, b) for b in range(1, STAY)]
    plan += [(beside_last, 0)]
    for step, p in plan:
        step(p)
    for j in range(RES_DEV):
        put(j, j)
    for l in range(MIG_DEV):
        k_of = 0
        for k in range(G):
            k_of = jnp.where(tab_s[k, 0] == RES_DEV + l, k, k_of)
        put(RES_DEV + k_of, RES_DEV + l)

    others = pl.ds(1, G - 1)
    over_g(zq.at[others], zq.at[others], zq_s.at[0], zq_r.at[0], g).wait_send()
    over_g(zrs.at[others], zrs.at[others], zs_s.at[0], zs_r.at[0], g).wait_send()
    over_g(zo.at[others], zo.at[others], zo_s.at[0], zo_r.at[0], g).wait_send()
    sent = qall.at[pl.ds(0, T - 1)]
    over_t(sent, sent, q_s.at[0], q_r.at[0], t).wait_send()
    stats, parts = rstat.at[:, rest], rbuf.at[:, rest]
    over_t(stats, stats, st_s.at[0], st_r.at[0], t).wait_send()
    over_t(parts, parts, o_s.at[0], o_r.at[0], t).wait_send()


def body(
    queries,
    new_entries,
    resident_cache,
    prefill_cache,
    resident_kept,
    kept_tokens,
    prefill_slot,
    decode_slot,
):
    G = lax.axis_size("group")
    T = lax.axis_size("tensor")
    KVL = max(1, KVH // T)
    HB = H // T
    RB = STEPS * HB
    R = RB // KVL
    LW = BATCH * R
    NB = STAY + G // BATCH
    PW = KVL * LW
    dma = pltpu.SemaphoreType.DMA
    vmem = pl.BlockSpec(memory_space=pltpu.VMEM)
    hbm = pl.BlockSpec(memory_space=pl.ANY)
    return pl.pallas_call(
        functools.partial(kernel, G, T),
        out_shape=pltpu.VMEM(queries.shape, BF16),
        in_specs=[hbm] * 8,
        out_specs=vmem,
        scratch_shapes=[
            pltpu.VMEM((3, kept_tokens.shape[0]), jnp.int32),
            pltpu.SMEM((1, resident_kept.shape[0]), jnp.int32),
            pltpu.VMEM((2 * G, 128), jnp.int32),
            pltpu.SMEM((2 * G, 128), jnp.int32),
            pltpu.VMEM(queries.shape, BF16),
            pltpu.VMEM(new_entries.shape, BF16),
            pltpu.VMEM((PER_GROUP, *resident_cache.shape[1:]), BF16),
            pltpu.VMEM((T, RES_DEV + G, RB, HD), BF16),
            pltpu.VMEM((G, RB, HD), BF16),
            pltpu.VMEM((PER_GROUP, RB, HD), F32),
            pltpu.VMEM((NB, T, KVL, LW, HD), BF16),
            pltpu.VMEM((NB, T, KVL, LW, HD), BF16),
            pltpu.VMEM((NB, T, 2, PW), F32),
            pltpu.VMEM((NB, T, 2, PW), F32),
            pltpu.VMEM((PW, 128), F32),
            pltpu.VMEM((2 * NB, -(-(T + 1) // 8) * 8, PW), F32),
            pltpu.VMEM((G, KVL, R, HD), BF16),
            pltpu.VMEM((G, KVL, R, HD), BF16),
            pltpu.VMEM((NB - STAY, 2, PW), F32),
            pltpu.VMEM((G, 2, PW), F32),
            pltpu.VMEM((NB, 2, KVL * BATCH * STEPS, HD), F32),
            pltpu.VMEM((NB, 2, PW), F32),
            pltpu.VMEM((NB, PW, HD), F32),
            pltpu.VMEM((NB * BATCH, RB, HD), F32),
            dma((5,)),
            pltpu.SemaphoreType.REGULAR((G // 2 if G & (G - 1) == 0 else G,)),
            pltpu.SemaphoreType.REGULAR((1,)),
            dma((1,)),
            dma((G,)),
            dma((1,)),
            dma((RES_DEV + G,)),
            dma((1,)),
            dma((NB,)),
            dma((1,)),
            dma((NB,)),
            dma((1,)),
            dma((NB - STAY,)),
            dma((1,)),
            dma((NB - STAY,)),
        ],
        compiler_params=pltpu.CompilerParams(collective_id=0, has_side_effects=True),
    )(
        kept_tokens[None],
        prefill_slot[None],
        decode_slot[None],
        resident_kept[None],
        queries, new_entries, resident_cache, prefill_cache)


def solution(mesh):
    in_specs = (
        P("group", None, "tensor"),
        P("group", None, None),
        P("group", "tensor", None),
        P("group", "tensor", None),
        P(),
        P(),
        P(),
        P(),
    )
    out_specs = P("group", None, "tensor")
    return jax.shard_map(body, mesh=mesh, in_specs=in_specs, out_specs=out_specs, check_vma=False)
```

```python
import functools
import math

import jax
import jax.numpy as jnp
from jax import lax
from jax.experimental import pallas as pl
from jax.experimental.pallas import tpu as pltpu
from jax.sharding import PartitionSpec as P

H = 64
KVH = 8
HD = 128
STEPS = 4
MIG_DEV = 8
RES_DEV = 4
PER_GROUP = RES_DEV + MIG_DEV
BATCH = 2
STAY = RES_DEV // BATCH

NEG_FLOOR = -1e30
SCALE = 1.0 / math.sqrt(HD)
MESH = pl.DeviceIdType.MESH
F32 = jnp.float32
BF16 = jnp.bfloat16
NT = (((1,), (1,)), ((), ()))
TN = (((0,), (0,)), ((), ()))


def flipped(v, mask):
    out, bit = v, 1
    while bit <= mask:
        if mask & bit:
            out = out + bit * (1 - 2 * lax.rem(lax.div(v, bit), 2))
        bit *= 2
    return out


def fill_table(peers, sources, g, plan_v, tab_v):
    G = len(peers)
    shape = (2 * G, plan_v.shape[1])
    n = lax.broadcasted_iota(jnp.int32, shape, 0)
    dest = jnp.broadcast_to(plan_v[2:3, :], shape)
    home = jnp.broadcast_to(plan_v[1:2, :], shape)
    kept = jnp.broadcast_to(plan_v[0:1, :], shape)
    dest_group, home_group = lax.div(dest, PER_GROUP), lax.div(home, MIG_DEV)
    other = jnp.zeros(shape, jnp.int32)
    for k in range(G):
        other = jnp.where(n == k, peers[k], other)
        other = jnp.where(n == G + k, sources[k], other)
    arriving = (n < G) & (dest_group == g) & (home_group == other)
    leaving = (n >= G) & (home_group == g) & (dest_group == other)
    picked = jnp.where(arriving, dest - dest_group * PER_GROUP, 0)
    held = home - home_group * MIG_DEV + MIG_DEV * kept
    picked = picked + jnp.where(leaving, held, 0)
    total = jnp.sum(picked, axis=1, keepdims=True)
    tab_v[...] = jnp.broadcast_to(total, tab_v.shape)


def kernel(
    G,
    T,
    kept_hbm,
    home_hbm,
    dest_hbm,
    stay_hbm,
    q_hbm,
    new_hbm,
    res_hbm,
    pre_hbm,
    out,
    plan_v,
    kept,
    tab_v,
    tab_s,
    q_in,
    new_in,
    cache,
    qall,
    zq,
    stage,
    obuf,
    rbuf,
    sbuf,
    rstat,
    statbuf,
    facbuf,
    zo,
    zro,
    zs,
    zrs,
    newk,
    nstat,
    nadd,
    fin,
    load_sem,
    above,
    across,
    zq_s,
    zq_r,
    q_s,
    q_r,
    o_s,
    o_r,
    st_s,
    st_r,
    zo_s,
    zo_r,
    zs_s,
    zs_r,
):
    KVL = max(1, KVH // T)
    HB = H // T
    HU = HB // KVL
    R = STEPS * HU
    LW = BATCH * R
    PW = KVL * LW
    NB = STAY + G // BATCH
    pos = cache.shape[1]
    half = KVH * HD
    g = lax.axis_index("group")
    t = lax.axis_index("tensor")
    offset = t * pos

    paired = G & (G - 1) == 0
    square = T == 4
    row_dev = t + 1 - 2 * lax.rem(t, 2)
    col_dev = t + 2 - 4 * lax.div(t, 2)
    greeted = (
        [(3, T - 1 - t), (2, col_dev), (1, row_dev)]
        if square
        else [(n, lax.rem(t + n, T)) for n in range(1, T)]
    )

    far_pairs = G // 2 - 1
    mine, beside = G - 1, G - 2

    def way(k):
        static = isinstance(k, int)
        if static and k >= beside:
            return mine - k
        pair = k // 2 if static else lax.div(k, 2)
        odd = k % 2 if static else lax.rem(k, 2)
        return 2 * (far_pairs - pair) + odd

    def at_way(mask):
        if not paired:
            return lax.rem(g + mask, G)
        out, bit = 0, 1
        while bit < G:
            a = lax.rem(lax.div(g, bit), 2)
            b = mask // bit % 2 if isinstance(mask, int) else lax.rem(lax.div(mask, bit), 2)
            out = out + bit * (a + b - 2 * a * b)
            bit *= 2
        return out

    def peer_g(k):
        return at_way(way(k))

    def from_g(k):
        return peer_g(k) if paired else at_way(G - way(k))

    level = lax.div(g, 2)
    first = far_pairs - lax.max(level, 1)

    def turn(i):
        if not paired:
            return i
        later = i - 1 + jnp.where(i > first, 1, 0)
        return jnp.where(i == 0, first, later)

    def turn_in(i):
        return jnp.where(first == far_pairs - 1, i, turn(i)) if paired else i

    def over_t(src, dst, ssem, rsem, dev):
        return pltpu.make_async_remote_copy(
            src_ref=src, dst_ref=dst, send_sem=ssem, recv_sem=rsem,
            device_id=(g, dev), device_id_type=MESH,
        )

    def over_g(src, dst, ssem, rsem, dev):
        return pltpu.make_async_remote_copy(
            src_ref=src, dst_ref=dst, send_sem=ssem, recv_sem=rsem,
            device_id=(dev, t), device_id_type=MESH,
        )

    def c_zq(k):
        return over_g(zq.at[k], qall.at[t, RES_DEV + k], zq_s.at[0], zq_r.at[k], peer_g(k))

    near = greeted[1:] if square else greeted

    def send_own(s, devs):
        own = qall.at[t, s]
        sem = place(s) if isinstance(s, int) else STAY + s - RES_DEV
        for _, dev in devs:
            over_t(own, own, q_s.at[0], q_r.at[sem], dev).start()

    def place(s):
        return s // BATCH if s < RES_DEV else STAY + s - RES_DEV

    def whole(k):
        rest = qall.at[pl.ds(0, T - 1), RES_DEV + k]
        over_t(rest, rest, q_s.at[0], q_r.at[STAY + k], t).wait_recv()

    def whole_stays(b):
        rest = qall.at[pl.ds(0, T - 1), pl.ds(b * BATCH, BATCH)]
        over_t(rest, rest, q_s.at[0], q_r.at[b], t).wait_recv()

    def c_o(b, j, n, p):
        rows = pl.ds(pl.multiple_of(j * R, R), R)
        return over_t(
            obuf.at[b, p, :, rows], rbuf.at[b, back(n), :, rows], o_s.at[0], o_r.at[b], p
        )

    def c_st(b, n, p):
        return over_t(sbuf.at[b, p], rstat.at[b, back(n)], st_s.at[0], st_r.at[b], p)

    def back(n):
        return n if square else T - n

    barrier = pltpu.get_barrier_semaphore()
    moving = [k for k in range(G) if k != mine]

    def when_above(k, act):
        @pl.when(peer_g(k) > g)
        def _():
            act()

    def when_below(k, act):
        @pl.when(peer_g(k) < g)
        def _():
            act()

    def greet(k):
        pl.semaphore_signal(barrier, inc=1, device_id=(peer_g(k), t), device_id_type=MESH)

    def answer(k):
        back = k if paired else [way(m) for m in range(G)].index((G - way(k)) % G)
        pl.semaphore_signal(
            above.at[back // 2 if paired else back], inc=1, device_id=(peer_g(k), t), device_id_type=MESH
        )

    def late(k):
        @pl.when(peer_g(k) > g)
        def _():
            if not paired:
                pl.semaphore_wait(above.at[k], 1)
            elif k % 2 == 0:
                pl.semaphore_wait(above.at[k // 2], 1 if k == beside else 2)
            c_zq(k).start()

    def meet():
        pl.semaphore_wait(barrier, g + len(near))
        for k in moving:
            when_below(k, functools.partial(answer, k))
        if square:
            pl.semaphore_signal(
                across.at[0], inc=1, device_id=(g, row_dev), device_id_type=MESH
            )

    for k in moving:
        when_above(k, functools.partial(greet, k))
    for _, dev in near:
        pl.semaphore_signal(barrier, inc=1, device_id=(g, dev), device_id_type=MESH)
    load_q = pltpu.make_async_copy(q_hbm, q_in, load_sem.at[2])
    load_new = pltpu.make_async_copy(new_hbm, new_in, load_sem.at[3])
    load_pre = pltpu.make_async_copy(pre_hbm, cache.at[0:MIG_DEV], load_sem.at[1])
    load_res = pltpu.make_async_copy(res_hbm, cache.at[MIG_DEV:PER_GROUP], load_sem.at[1])
    tables = [
        pltpu.make_async_copy(src, dst, load_sem.at[i // 3])
        for i, (src, dst) in enumerate(
            (
                (kept_hbm, plan_v.at[0:1]),
                (home_hbm, plan_v.at[1:2]),
                (dest_hbm, plan_v.at[2:3]),
                (stay_hbm, kept),
            )
        )
    ]
    for copy in tables:
        copy.start()
    load_q.start()
    load_new.start()
    meet()
    load_q.wait()

    def arrange(row):
        for h in range(HB):
            piece = q_in[row, :, h * HD : (h + 1) * HD]
            stage[row, h * STEPS : (h + 1) * STEPS, :] = piece.astype(F32)

    for j in range(RES_DEV):
        arrange(j)
        qall[t, j] = stage[j].astype(BF16)
    for j in range(RES_DEV):
        send_own(j, near)
    for row in range(RES_DEV, PER_GROUP):
        arrange(row)
    pltpu.make_async_copy(plan_v, plan_v, load_sem.at[0]).wait()
    tables[3].wait()
    load_pre.start()
    load_res.start()
    sources = [from_g(k) for k in range(G)]
    fill_table([peer_g(k) for k in range(G)], sources, g, plan_v, tab_v)
    load_tab = pltpu.make_async_copy(tab_v, tab_s, load_sem.at[2])
    load_tab.start()
    load_tab.wait()

    for k in range(G):
        block = stage[tab_s[k, 0]].astype(BF16)
        zq[k] = block
        if k == mine:
            qall[t, RES_DEV + k] = block

    for k in reversed(moving):
        when_below(k, c_zq(k).start)
    send_own(RES_DEV + mine, near)

    kv_col = pl.multiple_of((t * KVL * KVH) // (T * KVL) * HD, HD)

    def stage_new(b):
        for j in range(BATCH):
            row = b * BATCH + j if b < STAY else tab_s[(b - STAY) * BATCH + j, 0]
            for c in range(2):
                for i in range(KVL):
                    lo = (i * BATCH + j) * STEPS
                    col = pl.multiple_of(c * half + kv_col + i * HD, HD)
                    newk[b, c, lo : lo + STEPS, :] = new_in[row, :, pl.ds(col, HD)].astype(F32)

    def asked_of(b, j):
        return qall[t, b * BATCH + j] if b < STAY else zq[(b - STAY) * BATCH + j]

    r16 = lax.broadcasted_iota(jnp.int32, (KVL * BATCH * STEPS, PW), 0)
    lanes16 = lax.broadcasted_iota(jnp.int32, (KVL * BATCH * STEPS, PW), 1)
    causal = (r16 // STEPS == lanes16 // R) & (r16 % STEPS <= lanes16 % STEPS)

    def new_here(_):
        load_new.wait()

    def fresh(b):
        stage_new(b)
        asked = jnp.concatenate(
            [asked_of(b, j)[i * R : (i + 1) * R] for i in range(KVL) for j in range(BATCH)],
            axis=0,
        )
        keys, values = newk[b, 0].astype(BF16), newk[b, 1].astype(BF16)
        scores = lax.dot_general(keys, asked, NT, preferred_element_type=F32) * SCALE
        scores = jnp.where(causal, scores, NEG_FLOOR)
        top = jnp.max(scores, axis=0, keepdims=True)
        weights = jnp.where(causal, jnp.exp(scores - top), 0.0)
        nstat[b, 0:1, :] = top
        nstat[b, 1:2, :] = jnp.sum(weights, axis=0, keepdims=True)
        nadd[b] = lax.dot_general(
            weights.astype(BF16), values, TN, preferred_element_type=F32
        )

    def forward(k):
        came = qall.at[t, RES_DEV + k]
        over_g(came, came, zq_s.at[0], zq_r.at[k], g).wait_recv()
        send_own(RES_DEV + k, greeted)

    def attend_slot(row, length, slot, b, j, hold=False):
        lane = lax.broadcasted_iota(jnp.int32, (R, 128), 1)
        usable = offset + lax.broadcasted_iota(jnp.int32, (R, pos), 1) < length
        stats = [jnp.zeros((R, 128), F32) for _ in range(KVL)]
        rows = pl.ds(pl.multiple_of(j * R, R), R)
        W = 2 if KVL % 2 == 0 else 1
        units = [(tt, i) for tt in range(T) for i in range(0, KVL, W)]
        all_scores = []
        for tt, i in units:
            kv = (tt * KVL + i) * KVH // (T * KVL)
            asked = qall[tt, slot, i * R : (i + W) * R, :]
            keys = jnp.concatenate(
                [cache[row, :, (kv + w) * HD : (kv + w + 1) * HD] for w in range(W)], axis=0
            )
            scores = lax.dot_general(asked, keys, NT, preferred_element_type=F32)
            all_scores.append(
                [scores[w * R : (w + 1) * R, w * pos : (w + 1) * pos] * SCALE for w in range(W)]
            )
        all_weights = []
        for (tt, i), scores in zip(units, all_scores):
            rounded = []
            for w in range(W):
                masked = jnp.where(usable, scores[w], NEG_FLOOR)
                highest = jnp.max(masked, axis=1, keepdims=True)
                weights = jnp.where(usable, jnp.exp(masked - highest), 0.0)
                total = jnp.sum(weights, axis=1, keepdims=True)
                rounded.append(weights.astype(BF16))
                stats[i + w] = jnp.where(lane == 2 * tt, highest, stats[i + w])
                stats[i + w] = jnp.where(lane == 2 * tt + 1, total, stats[i + w])
            all_weights.append(jnp.concatenate(rounded, axis=0))
        for (tt, i), weights in zip(units, all_weights):
            kv = (tt * KVL + i) * KVH // (T * KVL)
            values = cache[row, :, half + kv * HD : half + (kv + W) * HD]
            blended = jnp.dot(weights, values, preferred_element_type=F32)
            for w in range(W):
                obuf[b, tt, i + w, rows, :] = blended[
                    w * R : (w + 1) * R, w * HD : (w + 1) * HD
                ].astype(BF16)
        for i in range(KVL):
            statbuf[pl.ds(pl.multiple_of(i * LW + j * R, R), R), :] = stats[i]
        if not hold:
            for n, p in greeted:
                c_o(b, j, n, p).start()

    def send_stats(b):
        for n, p in greeted:
            c_st(b, n, p).start()
        rbuf[b, 0] = obuf[b, t]
        rstat[b, 0] = sbuf[b, t]

    rest = pl.ds(1, T - 1)

    def loaded(_):
        pltpu.make_async_copy(cache, cache, load_sem.at[1]).wait()

    def turn_stats(b):
        turned = statbuf[...].T
        for tt in range(T):
            sbuf[b, tt] = turned[2 * tt : 2 * tt + 2, :]

    def stay_batch(b, hold=True):
        whole_stays(b)

        @pl.loop(0, BATCH)
        def _(j):
            s = b * BATCH + j
            attend_slot(MIG_DEV + s, kept[0, g * RES_DEV + s], s, b, j, hold)

        turn_stats(b)
        if not hold:
            send_stats(b)

    def moved_batch(b, hold=False):
        @pl.loop(0, BATCH)
        def _(j):
            k = (b - STAY) * BATCH + j
            whole(k)
            held = tab_s[G + k, 0]
            attend_slot(held % MIG_DEV, held // MIG_DEV, RES_DEV + k, b, j, hold)

        turn_stats(b)
        if not hold:
            send_stats(b)

    def send_batch(b):
        for j in range(BATCH):
            for n, p in greeted:
                c_o(b, j, n, p).start()
        send_stats(b)

    def reach(_):
        if square:
            pl.semaphore_wait(across.at[0], 1)
            for s in (*range(RES_DEV), RES_DEV + mine):
                send_own(s, greeted[:1])

    def stays():
        pl.loop(0, STAY)(stay_batch)

    def locals_held(_):
        moved_batch(NB - 1, True)

    def far(_):
        @pl.loop(0, far_pairs)
        def _(i):
            moved_batch(STAY + turn(i))

    def forward_pair(i):
        for j in range(2):
            forward(2 * turn_in(i) + j)

    def forward_rest(_):
        pl.loop(1, far_pairs - 1)(forward_pair)


    F, N, L = forward, fresh, late
    middle = list(range(2, beside))
    early = g < G // 4

    def stays_early(_):
        @pl.when(early)
        def _():
            stay_batch(0, False)
            pl.loop(1, STAY)(stay_batch)

    def first_stay_late(_):
        @pl.when(jnp.logical_not(early))
        def _():
            stay_batch(0)

    def stays_late(_):
        @pl.when(jnp.logical_not(early))
        def _():
            pl.loop(1, STAY)(stay_batch)

    def held_late(_):
        pl.when(jnp.logical_not(early))(functools.partial(send_batch, 0))
        for b in range(1, STAY):
            send_batch(b)

    plan = [(new_here, 0), (N, 0), (reach, 0), (L, beside), (L, beside - 2), (L, beside - 1), (F, beside)]
    plan += [(N, 1)] + [(L, k + j) for k in reversed(range(0, beside - 2, 2)) for j in range(2)] + [(N, NB - 1)]
    plan += [(F, beside - 2), (F, beside - 1), (loaded, 0), (stays_early, 0)]
    plan += [(forward_pair, 0), (first_stay_late, 0), (forward_rest, 0)]
    plan += [(stays_late, 0), (locals_held, 0), (far, 0), (send_batch, NB - 1)]
    plan += [(held_late, 0)]
    plan += [(N, b) for b in range(STAY, NB - 1)]
    for step, p in plan:
        step(p)

    def arrived(b):
        over_t(rstat.at[b, rest], rstat.at[b, rest], st_s.at[0], st_r.at[b], t).wait_recv()
        over_t(rbuf.at[b, rest], rbuf.at[b, rest], o_s.at[0], o_r.at[b], t).wait_recv()

    def factors_of(b):
        tops = [rstat[b, n][0:1] for n in range(T)]
        highest = functools.reduce(jnp.maximum, tops)
        factors = [jnp.exp(top - highest) for top in tops]
        total = factors[0] * rstat[b, 0][1:2]
        for n in range(1, T):
            total = total + factors[n] * rstat[b, n][1:2]
        return highest, total, factors

    def columns_of(place, rows):
        for i, row in enumerate(rows):
            facbuf[place, i : i + 1, :] = row
        return facbuf[place].T

    def blend(b, columns):
        blended = rbuf[b, 0].reshape(PW, HD).astype(F32) * columns[:, 0:1]
        for n in range(1, T):
            blended = blended + rbuf[b, n].reshape(PW, HD).astype(F32) * columns[:, n : n + 1]
        return blended

    def merged(b):
        highest, total, factors = factors_of(b)
        return highest, total, blend(b, columns_of(b, factors))

    def with_new(b, highest, total):
        top = jnp.maximum(highest, nstat[b, 0:1])
        old_part, new_part = jnp.exp(highest - top), jnp.exp(nstat[b, 0:1] - top)
        inverse = 1.0 / (total * old_part + nstat[b, 1:2] * new_part)
        return old_part * inverse, new_part * inverse

    def keep(b, done):
        for j in range(BATCH):
            for i in range(KVL):
                lo = i * LW + j * R
                fin[b * BATCH + j, i * R : (i + 1) * R, :] = done[lo : lo + R]

    def finish(b, highest, total, blended):
        columns = columns_of(NB + b, with_new(b, highest, total))
        keep(b, blended * columns[:, 0:1] + nadd[b] * columns[:, 1:2])

    def put(slot, row):
        for h in range(HB):
            piece = fin[slot, h * STEPS : (h + 1) * STEPS, :]
            out[row, :, h * HD : (h + 1) * HD] = piece.astype(BF16)

    def give_back(b):
        arrived(b)
        highest, total, blended = merged(b)
        zs[b - STAY] = jnp.concatenate([highest, total], axis=0)
        for j in range(BATCH):
            k = (b - STAY) * BATCH + j
            for i in range(KVL):
                zo[k, i] = blended[i * LW + j * R : i * LW + (j + 1) * R].astype(BF16)
            if isinstance(k, int) and k == mine:
                zrs[k] = zs[b - STAY]
                zro[k] = zo[k]
            else:
                pair, dev = b - STAY, from_g(k)
                over_g(zs.at[pair], zrs.at[k], zs_s.at[0], zs_r.at[pair], dev).start()
                over_g(zo.at[k], zro.at[k], zo_s.at[0], zo_r.at[pair], dev).start()

    def give_far(_):
        @pl.loop(0, far_pairs)
        def _(i):
            give_back(STAY + turn(i))

    def end_stay(b):
        highest, total, factors = factors_of(b)
        old, new = with_new(b, highest, total)
        columns = columns_of(b, [factor * old for factor in factors] + [new])
        keep(b, blend(b, columns) + nadd[b] * columns[:, T : T + 1])

    def returned(b):
        first = (b - STAY) * BATCH
        came = pl.ds(first, BATCH - (first <= mine < first + BATCH))
        over_g(zrs.at[came], zrs.at[came], zs_s.at[0], zs_r.at[b - STAY], g).wait_recv()
        over_g(zro.at[came], zro.at[came], zo_s.at[0], zo_r.at[b - STAY], g).wait_recv()

    def end_moved(b):
        lanes = lax.broadcasted_iota(jnp.int32, (2, PW), 1)
        stats = jnp.zeros((2, PW), F32)
        first = (b - STAY) * BATCH
        for j in range(BATCH):
            stats = jnp.where((lanes // R) % BATCH == j, zrs[first + j], stats)
        blended = jnp.concatenate(
            [zro[first + j, i].astype(F32) for i in range(KVL) for j in range(BATCH)], axis=0
        )
        finish(b, stats[0:1], stats[1:2], blended)

    slots = []
    for l in range(MIG_DEV):
        k_of = 0
        for k in range(G):
            k_of = jnp.where(tab_s[k, 0] == RES_DEV + l, k, k_of)
        slots.append(k_of)

    moved = list(range(STAY, NB))
    def stay_early(_):
        @pl.when(early)
        def _():
            arrived(0)
            end_stay(0)

    def stay_late(_):
        @pl.when(jnp.logical_not(early))
        def _():
            arrived(0)
            end_stay(0)

    plan = [(stay_early, 0), (give_far, 0), (give_back, moved[-1]), (stay_late, 0)]
    waits_long = early & (lax.rem(g, 2) == 1)

    def end_beside(_):
        returned(moved[-1])
        end_moved(moved[-1])

    def beside_soon(_):
        pl.when(jnp.logical_not(waits_long))(functools.partial(end_beside, 0))

    def beside_last(_):
        pl.when(waits_long)(functools.partial(end_beside, 0))

    plan += [(returned, b) for b in moved[1:-1]] + [(end_moved, b) for b in moved[1:-1]]
    plan += [(beside_soon, 0), (returned, moved[0])] + [(arrived, b) for b in range(1, STAY)]
    plan += [(end_moved, moved[0])] + [(end_stay, b) for b in range(1, STAY)]
    plan += [(beside_last, 0)]
    for step, p in plan:
        step(p)
    for j in range(RES_DEV):
        put(j, j)
    for l in range(MIG_DEV):
        put(RES_DEV + slots[l], RES_DEV + l)

    others = pl.ds(1, G - 1)
    over_g(zq.at[others], zq.at[others], zq_s.at[0], zq_r.at[0], g).wait_send()
    over_g(zrs.at[others], zrs.at[others], zs_s.at[0], zs_r.at[0], g).wait_send()
    over_g(zo.at[others], zo.at[others], zo_s.at[0], zo_r.at[0], g).wait_send()
    sent = qall.at[pl.ds(0, T - 1)]
    over_t(sent, sent, q_s.at[0], q_r.at[0], t).wait_send()
    stats, parts = rstat.at[:, rest], rbuf.at[:, rest]
    over_t(stats, stats, st_s.at[0], st_r.at[0], t).wait_send()
    over_t(parts, parts, o_s.at[0], o_r.at[0], t).wait_send()


def body(
    queries,
    new_entries,
    resident_cache,
    prefill_cache,
    resident_kept,
    kept_tokens,
    prefill_slot,
    decode_slot,
):
    G = lax.axis_size("group")
    T = lax.axis_size("tensor")
    KVL = max(1, KVH // T)
    HB = H // T
    RB = STEPS * HB
    R = RB // KVL
    LW = BATCH * R
    NB = STAY + G // BATCH
    PW = KVL * LW
    dma = pltpu.SemaphoreType.DMA
    vmem = pl.BlockSpec(memory_space=pltpu.VMEM)
    hbm = pl.BlockSpec(memory_space=pl.ANY)
    return pl.pallas_call(
        functools.partial(kernel, G, T),
        out_shape=pltpu.VMEM(queries.shape, BF16),
        in_specs=[hbm] * 8,
        out_specs=vmem,
        scratch_shapes=[
            pltpu.VMEM((3, kept_tokens.shape[0]), jnp.int32),
            pltpu.SMEM((1, resident_kept.shape[0]), jnp.int32),
            pltpu.VMEM((2 * G, 128), jnp.int32),
            pltpu.SMEM((2 * G, 128), jnp.int32),
            pltpu.VMEM(queries.shape, BF16),
            pltpu.VMEM(new_entries.shape, BF16),
            pltpu.VMEM((PER_GROUP, *resident_cache.shape[1:]), BF16),
            pltpu.VMEM((T, RES_DEV + G, RB, HD), BF16),
            pltpu.VMEM((G, RB, HD), BF16),
            pltpu.VMEM((PER_GROUP, RB, HD), F32),
            pltpu.VMEM((NB, T, KVL, LW, HD), BF16),
            pltpu.VMEM((NB, T, KVL, LW, HD), BF16),
            pltpu.VMEM((NB, T, 2, PW), F32),
            pltpu.VMEM((NB, T, 2, PW), F32),
            pltpu.VMEM((PW, 128), F32),
            pltpu.VMEM((2 * NB, -(-(T + 1) // 8) * 8, PW), F32),
            pltpu.VMEM((G, KVL, R, HD), BF16),
            pltpu.VMEM((G, KVL, R, HD), BF16),
            pltpu.VMEM((NB - STAY, 2, PW), F32),
            pltpu.VMEM((G, 2, PW), F32),
            pltpu.VMEM((NB, 2, KVL * BATCH * STEPS, HD), F32),
            pltpu.VMEM((NB, 2, PW), F32),
            pltpu.VMEM((NB, PW, HD), F32),
            pltpu.VMEM((NB * BATCH, RB, HD), F32),
            dma((4,)),
            pltpu.SemaphoreType.REGULAR((G // 2 if G & (G - 1) == 0 else G,)),
            pltpu.SemaphoreType.REGULAR((1,)),
            dma((1,)),
            dma((G - 1,)),
            dma((1,)),
            dma((STAY + G,)),
            dma((1,)),
            dma((NB,)),
            dma((1,)),
            dma((NB,)),
            dma((1,)),
            dma((NB - STAY,)),
            dma((1,)),
            dma((NB - STAY,)),
        ],
        compiler_params=pltpu.CompilerParams(collective_id=0, has_side_effects=True),
    )(
        kept_tokens[None],
        prefill_slot[None],
        decode_slot[None],
        resident_kept[None],
        queries, new_entries, resident_cache, prefill_cache)


def solution(mesh):
    in_specs = (
        P("group", None, "tensor"),
        P("group", None, None),
        P("group", "tensor", None),
        P("group", "tensor", None),
        P(),
        P(),
        P(),
        P(),
    )
    out_specs = P("group", None, "tensor")
    return jax.shard_map(body, mesh=mesh, in_specs=in_specs, out_specs=out_specs, check_vma=False)
```

```python
import functools
import math

import jax
import jax.numpy as jnp
from jax import lax
from jax.experimental import pallas as pl
from jax.experimental.pallas import tpu as pltpu
from jax.sharding import PartitionSpec as P

H = 64
KVH = 8
HD = 128
STEPS = 4
MIG_DEV = 8
RES_DEV = 4
PER_GROUP = RES_DEV + MIG_DEV
BATCH = 2
STAY = RES_DEV // BATCH

NEG_FLOOR = -1e30
SCALE = 1.0 / math.sqrt(HD)
MESH = pl.DeviceIdType.MESH
F32 = jnp.float32
BF16 = jnp.bfloat16
NT = (((1,), (1,)), ((), ()))
TN = (((0,), (0,)), ((), ()))


def flipped(v, mask):
    out, bit = v, 1
    while bit <= mask:
        if mask & bit:
            out = out + bit * (1 - 2 * lax.rem(lax.div(v, bit), 2))
        bit *= 2
    return out


def fill_table(peers, sources, g, plan_v, tab_v):
    G = len(peers)
    shape = (2 * G, plan_v.shape[1])
    n = lax.broadcasted_iota(jnp.int32, shape, 0)
    dest = jnp.broadcast_to(plan_v[2:3, :], shape)
    home = jnp.broadcast_to(plan_v[1:2, :], shape)
    kept = jnp.broadcast_to(plan_v[0:1, :], shape)
    dest_group, home_group = lax.div(dest, PER_GROUP), lax.div(home, MIG_DEV)
    other = jnp.zeros(shape, jnp.int32)
    for k in range(G):
        other = jnp.where(n == k, peers[k], other)
        other = jnp.where(n == G + k, sources[k], other)
    arriving = (n < G) & (dest_group == g) & (home_group == other)
    leaving = (n >= G) & (home_group == g) & (dest_group == other)
    picked = jnp.where(arriving, dest - dest_group * PER_GROUP, 0)
    held = home - home_group * MIG_DEV + MIG_DEV * kept
    picked = picked + jnp.where(leaving, held, 0)
    total = jnp.sum(picked, axis=1, keepdims=True)
    tab_v[...] = jnp.broadcast_to(total, tab_v.shape)


def kernel(
    G,
    T,
    kept_hbm,
    home_hbm,
    dest_hbm,
    stay_hbm,
    q_hbm,
    new_hbm,
    res_hbm,
    pre_hbm,
    out,
    plan_v,
    kept,
    tab_v,
    tab_s,
    q_in,
    new_in,
    cache,
    qall,
    zq,
    stage,
    obuf,
    rbuf,
    sbuf,
    rstat,
    statbuf,
    facbuf,
    zo,
    zro,
    zs,
    zrs,
    newk,
    nstat,
    nadd,
    fin,
    load_sem,
    above,
    across,
    zq_s,
    zq_r,
    q_s,
    q_r,
    o_s,
    o_r,
    st_s,
    st_r,
    zo_s,
    zo_r,
    zs_s,
    zs_r,
):
    KVL = max(1, KVH // T)
    HB = H // T
    HU = HB // KVL
    R = STEPS * HU
    LW = BATCH * R
    PW = KVL * LW
    NB = STAY + G // BATCH
    pos = cache.shape[1]
    half = KVH * HD
    g = lax.axis_index("group")
    t = lax.axis_index("tensor")
    offset = t * pos

    paired = G & (G - 1) == 0
    square = T == 4
    row_dev = t + 1 - 2 * lax.rem(t, 2)
    col_dev = t + 2 - 4 * lax.div(t, 2)
    greeted = (
        [(3, T - 1 - t), (2, col_dev), (1, row_dev)]
        if square
        else [(n, lax.rem(t + n, T)) for n in range(1, T)]
    )

    far_pairs = G // 2 - 1
    mine, beside = G - 1, G - 2

    def way(k):
        static = isinstance(k, int)
        if static and k >= beside:
            return mine - k
        pair = k // 2 if static else lax.div(k, 2)
        odd = k % 2 if static else lax.rem(k, 2)
        return 2 * (far_pairs - pair) + odd

    def at_way(mask):
        if not paired:
            return lax.rem(g + mask, G)
        out, bit = 0, 1
        while bit < G:
            a = lax.rem(lax.div(g, bit), 2)
            b = mask // bit % 2 if isinstance(mask, int) else lax.rem(lax.div(mask, bit), 2)
            out = out + bit * (a + b - 2 * a * b)
            bit *= 2
        return out

    def peer_g(k):
        return at_way(way(k))

    def from_g(k):
        return peer_g(k) if paired else at_way(G - way(k))

    level = lax.div(g, 2)
    first = far_pairs - lax.max(level, 1)

    def turn(i):
        if not paired:
            return i
        later = i - 1 + jnp.where(i > first, 1, 0)
        return jnp.where(i == 0, first, later)

    def turn_in(i):
        return jnp.where(first == far_pairs - 1, i, turn(i)) if paired else i

    def over_t(src, dst, ssem, rsem, dev):
        return pltpu.make_async_remote_copy(
            src_ref=src, dst_ref=dst, send_sem=ssem, recv_sem=rsem,
            device_id=(g, dev), device_id_type=MESH,
        )

    def over_g(src, dst, ssem, rsem, dev):
        return pltpu.make_async_remote_copy(
            src_ref=src, dst_ref=dst, send_sem=ssem, recv_sem=rsem,
            device_id=(dev, t), device_id_type=MESH,
        )

    def c_zq(k):
        return over_g(zq.at[k], qall.at[t, RES_DEV + k], zq_s.at[0], zq_r.at[k], peer_g(k))

    near = greeted[1:] if square else greeted

    def send_own(s, devs):
        own = qall.at[t, s]
        for _, dev in devs:
            over_t(own, own, q_s.at[0], q_r.at[s], dev).start()

    def whole(s):
        rest = qall.at[pl.ds(0, T - 1), s]
        over_t(rest, rest, q_s.at[0], q_r.at[s], t).wait_recv()

    def c_o(b, j, n, p):
        rows = pl.ds(pl.multiple_of(j * R, R), R)
        return over_t(
            obuf.at[b, p, :, rows], rbuf.at[b, back(n), :, rows], o_s.at[0], o_r.at[b], p
        )

    def c_st(b, n, p):
        return over_t(sbuf.at[b, p], rstat.at[b, back(n)], st_s.at[0], st_r.at[b], p)

    def back(n):
        return n if square else T - n

    barrier = pltpu.get_barrier_semaphore()
    moving = [k for k in range(G) if k != mine]

    def when_above(k, act):
        @pl.when(peer_g(k) > g)
        def _():
            act()

    def when_below(k, act):
        @pl.when(peer_g(k) < g)
        def _():
            act()

    def greet(k):
        pl.semaphore_signal(barrier, inc=1, device_id=(peer_g(k), t), device_id_type=MESH)

    def answer(k):
        back = k if paired else [way(m) for m in range(G)].index((G - way(k)) % G)
        pl.semaphore_signal(
            above.at[back // 2 if paired else back], inc=1, device_id=(peer_g(k), t), device_id_type=MESH
        )

    def late(k):
        @pl.when(peer_g(k) > g)
        def _():
            if not paired:
                pl.semaphore_wait(above.at[k], 1)
            elif k % 2 == 0:
                pl.semaphore_wait(above.at[k // 2], 1 if k == beside else 2)
            c_zq(k).start()

    def meet():
        pl.semaphore_wait(barrier, g + len(near))
        for k in moving:
            when_below(k, functools.partial(answer, k))
        if square:
            pl.semaphore_signal(
                across.at[0], inc=1, device_id=(g, row_dev), device_id_type=MESH
            )

    for k in moving:
        when_above(k, functools.partial(greet, k))
    for _, dev in near:
        pl.semaphore_signal(barrier, inc=1, device_id=(g, dev), device_id_type=MESH)
    load_q = pltpu.make_async_copy(q_hbm, q_in, load_sem.at[2])
    load_new = pltpu.make_async_copy(new_hbm, new_in, load_sem.at[3])
    load_pre = pltpu.make_async_copy(pre_hbm, cache.at[0:MIG_DEV], load_sem.at[4])
    load_res = pltpu.make_async_copy(res_hbm, cache.at[MIG_DEV:PER_GROUP], load_sem.at[4])
    tables = [
        pltpu.make_async_copy(src, dst, load_sem.at[i // 3])
        for i, (src, dst) in enumerate(
            (
                (kept_hbm, plan_v.at[0:1]),
                (home_hbm, plan_v.at[1:2]),
                (dest_hbm, plan_v.at[2:3]),
                (stay_hbm, kept),
            )
        )
    ]
    for copy in tables:
        copy.start()
    load_q.start()
    load_new.start()
    meet()
    load_q.wait()

    def arrange(row):
        for h in range(HB):
            piece = q_in[row, :, h * HD : (h + 1) * HD]
            stage[row, h * STEPS : (h + 1) * STEPS, :] = piece.astype(F32)

    for j in range(RES_DEV):
        arrange(j)
        qall[t, j] = stage[j].astype(BF16)
    for j in range(RES_DEV):
        send_own(j, near)
    for row in range(RES_DEV, PER_GROUP):
        arrange(row)
    pltpu.make_async_copy(plan_v, plan_v, load_sem.at[0]).wait()
    tables[3].wait()
    load_pre.start()
    load_res.start()
    sources = [from_g(k) for k in range(G)]
    fill_table([peer_g(k) for k in range(G)], sources, g, plan_v, tab_v)
    load_tab = pltpu.make_async_copy(tab_v, tab_s, load_sem.at[2])
    load_tab.start()
    load_tab.wait()

    for k in range(G):
        block = stage[tab_s[k, 0]].astype(BF16)
        zq[k] = block
        if k == mine:
            qall[t, RES_DEV + k] = block

    for k in reversed(moving):
        when_below(k, c_zq(k).start)
    send_own(RES_DEV + mine, near)

    kv_col = pl.multiple_of((t * KVL * KVH) // (T * KVL) * HD, HD)

    def stage_new(b):
        for j in range(BATCH):
            row = b * BATCH + j if b < STAY else tab_s[(b - STAY) * BATCH + j, 0]
            for c in range(2):
                for i in range(KVL):
                    lo = (i * BATCH + j) * STEPS
                    col = pl.multiple_of(c * half + kv_col + i * HD, HD)
                    newk[b, c, lo : lo + STEPS, :] = new_in[row, :, pl.ds(col, HD)].astype(F32)

    def asked_of(b, j):
        return qall[t, b * BATCH + j] if b < STAY else zq[(b - STAY) * BATCH + j]

    r16 = lax.broadcasted_iota(jnp.int32, (KVL * BATCH * STEPS, PW), 0)
    lanes16 = lax.broadcasted_iota(jnp.int32, (KVL * BATCH * STEPS, PW), 1)
    causal = (r16 // STEPS == lanes16 // R) & (r16 % STEPS <= lanes16 % STEPS)

    def new_here(_):
        load_new.wait()

    def fresh(b):
        stage_new(b)
        asked = jnp.concatenate(
            [asked_of(b, j)[i * R : (i + 1) * R] for i in range(KVL) for j in range(BATCH)],
            axis=0,
        )
        keys, values = newk[b, 0].astype(BF16), newk[b, 1].astype(BF16)
        scores = lax.dot_general(keys, asked, NT, preferred_element_type=F32) * SCALE
        scores = jnp.where(causal, scores, NEG_FLOOR)
        top = jnp.max(scores, axis=0, keepdims=True)
        weights = jnp.where(causal, jnp.exp(scores - top), 0.0)
        nstat[b, 0:1, :] = top
        nstat[b, 1:2, :] = jnp.sum(weights, axis=0, keepdims=True)
        nadd[b] = lax.dot_general(
            weights.astype(BF16), values, TN, preferred_element_type=F32
        )

    def forward(k):
        came = qall.at[t, RES_DEV + k]
        over_g(came, came, zq_s.at[0], zq_r.at[k], g).wait_recv()
        send_own(RES_DEV + k, greeted)

    def attend_slot(row, length, slot, b, j, hold=False):
        lane = lax.broadcasted_iota(jnp.int32, (R, 128), 1)
        usable = offset + lax.broadcasted_iota(jnp.int32, (R, pos), 1) < length
        stats = [jnp.zeros((R, 128), F32) for _ in range(KVL)]
        rows = pl.ds(pl.multiple_of(j * R, R), R)
        W = 2 if KVL % 2 == 0 else 1
        units = [(tt, i) for tt in range(T) for i in range(0, KVL, W)]
        all_scores = []
        for tt, i in units:
            kv = (tt * KVL + i) * KVH // (T * KVL)
            parts = [qall[tt, slot, (i + w) * R : (i + w + 1) * R, :] for w in range(W)]
            blank = jnp.zeros((R, HD), BF16)
            asked = jnp.concatenate(
                [
                    jnp.concatenate([parts[w] if v == w else blank for v in range(W)], axis=1)
                    for w in range(W)
                ],
                axis=0,
            )
            keys = cache[row, :, kv * HD : (kv + W) * HD]
            scores = lax.dot_general(asked, keys, NT, preferred_element_type=F32)
            all_scores.append([scores[w * R : (w + 1) * R] * SCALE for w in range(W)])
        all_weights = []
        for (tt, i), scores in zip(units, all_scores):
            rounded = []
            for w in range(W):
                masked = jnp.where(usable, scores[w], NEG_FLOOR)
                highest = jnp.max(masked, axis=1, keepdims=True)
                weights = jnp.where(usable, jnp.exp(masked - highest), 0.0)
                total = jnp.sum(weights, axis=1, keepdims=True)
                rounded.append(weights.astype(BF16))
                stats[i + w] = jnp.where(lane == 2 * tt, highest, stats[i + w])
                stats[i + w] = jnp.where(lane == 2 * tt + 1, total, stats[i + w])
            all_weights.append(jnp.concatenate(rounded, axis=0))
        for (tt, i), weights in zip(units, all_weights):
            kv = (tt * KVL + i) * KVH // (T * KVL)
            values = cache[row, :, half + kv * HD : half + (kv + W) * HD]
            blended = jnp.dot(weights, values, preferred_element_type=F32)
            for w in range(W):
                obuf[b, tt, i + w, rows, :] = blended[
                    w * R : (w + 1) * R, w * HD : (w + 1) * HD
                ].astype(BF16)
        for i in range(KVL):
            statbuf[pl.ds(pl.multiple_of(i * LW + j * R, R), R), :] = stats[i]
        if not hold:
            for n, p in greeted:
                c_o(b, j, n, p).start()

    def send_stats(b):
        for n, p in greeted:
            c_st(b, n, p).start()
        rbuf[b, 0] = obuf[b, t]
        rstat[b, 0] = sbuf[b, t]

    rest = pl.ds(1, T - 1)

    def loaded(_):
        pltpu.make_async_copy(cache, cache, load_sem.at[4]).wait()

    def turn_stats(b):
        turned = statbuf[...].T
        for tt in range(T):
            sbuf[b, tt] = turned[2 * tt : 2 * tt + 2, :]

    def stay_batch(b, hold=True):
        @pl.loop(0, BATCH)
        def _(j):
            s = b * BATCH + j
            whole(s)
            attend_slot(MIG_DEV + s, kept[0, g * RES_DEV + s], s, b, j, hold)

        turn_stats(b)
        if not hold:
            send_stats(b)

    def moved_batch(b, hold=False):
        @pl.loop(0, BATCH)
        def _(j):
            k = (b - STAY) * BATCH + j
            whole(RES_DEV + k)
            held = tab_s[G + k, 0]
            attend_slot(held % MIG_DEV, held // MIG_DEV, RES_DEV + k, b, j, hold)

        turn_stats(b)
        if not hold:
            send_stats(b)

    def send_batch(b):
        for j in range(BATCH):
            for n, p in greeted:
                c_o(b, j, n, p).start()
        send_stats(b)

    def reach(_):
        if square:
            pl.semaphore_wait(across.at[0], 1)
            for s in (*range(RES_DEV), RES_DEV + mine):
                send_own(s, greeted[:1])

    def stays():
        pl.loop(0, STAY)(stay_batch)

    def locals_held(_):
        moved_batch(NB - 1, True)

    def far(_):
        @pl.loop(0, far_pairs)
        def _(i):
            moved_batch(STAY + turn(i))

    def forward_pair(i):
        for j in range(2):
            forward(2 * turn_in(i) + j)

    def forward_rest(_):
        pl.loop(1, far_pairs - 1)(forward_pair)


    F, N, L = forward, fresh, late
    middle = list(range(2, beside))
    early = g < G // 4

    def stays_early(_):
        @pl.when(early)
        def _():
            stay_batch(0, False)
            pl.loop(1, STAY)(stay_batch)

    def first_stay_late(_):
        @pl.when(jnp.logical_not(early))
        def _():
            stay_batch(0)

    def stays_late(_):
        @pl.when(jnp.logical_not(early))
        def _():
            pl.loop(1, STAY)(stay_batch)

    def held_late(_):
        pl.when(jnp.logical_not(early))(functools.partial(send_batch, 0))
        for b in range(1, STAY):
            send_batch(b)

    plan = [(new_here, 0), (N, 0), (reach, 0), (L, beside), (L, beside - 2), (L, beside - 1), (F, beside)]
    plan += [(N, 1)] + [(L, k + j) for k in reversed(range(0, beside - 2, 2)) for j in range(2)] + [(N, NB - 1)]
    plan += [(F, beside - 2), (F, beside - 1), (loaded, 0), (stays_early, 0)]
    plan += [(forward_pair, 0), (first_stay_late, 0), (forward_rest, 0)]
    plan += [(stays_late, 0), (locals_held, 0), (far, 0), (send_batch, NB - 1)]
    plan += [(held_late, 0)]
    plan += [(N, b) for b in range(STAY, NB - 1)]
    for step, p in plan:
        step(p)

    def arrived(b):
        over_t(rstat.at[b, rest], rstat.at[b, rest], st_s.at[0], st_r.at[b], t).wait_recv()
        over_t(rbuf.at[b, rest], rbuf.at[b, rest], o_s.at[0], o_r.at[b], t).wait_recv()

    def factors_of(b):
        tops = [rstat[b, n][0:1] for n in range(T)]
        highest = functools.reduce(jnp.maximum, tops)
        factors = [jnp.exp(top - highest) for top in tops]
        total = factors[0] * rstat[b, 0][1:2]
        for n in range(1, T):
            total = total + factors[n] * rstat[b, n][1:2]
        return highest, total, factors

    def columns_of(place, rows):
        for i, row in enumerate(rows):
            facbuf[place, i : i + 1, :] = row
        return facbuf[place].T

    def blend(b, columns):
        blended = rbuf[b, 0].reshape(PW, HD).astype(F32) * columns[:, 0:1]
        for n in range(1, T):
            blended = blended + rbuf[b, n].reshape(PW, HD).astype(F32) * columns[:, n : n + 1]
        return blended

    def merged(b):
        highest, total, factors = factors_of(b)
        return highest, total, blend(b, columns_of(b, factors))

    def with_new(b, highest, total):
        top = jnp.maximum(highest, nstat[b, 0:1])
        old_part, new_part = jnp.exp(highest - top), jnp.exp(nstat[b, 0:1] - top)
        inverse = 1.0 / (total * old_part + nstat[b, 1:2] * new_part)
        return old_part * inverse, new_part * inverse

    def keep(b, done):
        for j in range(BATCH):
            for i in range(KVL):
                lo = i * LW + j * R
                fin[b * BATCH + j, i * R : (i + 1) * R, :] = done[lo : lo + R]

    def finish(b, highest, total, blended):
        columns = columns_of(NB + b, with_new(b, highest, total))
        keep(b, blended * columns[:, 0:1] + nadd[b] * columns[:, 1:2])

    def put(slot, row):
        for h in range(HB):
            piece = fin[slot, h * STEPS : (h + 1) * STEPS, :]
            out[row, :, h * HD : (h + 1) * HD] = piece.astype(BF16)

    def give_back(b):
        arrived(b)
        highest, total, blended = merged(b)
        zs[b - STAY] = jnp.concatenate([highest, total], axis=0)
        for j in range(BATCH):
            k = (b - STAY) * BATCH + j
            for i in range(KVL):
                zo[k, i] = blended[i * LW + j * R : i * LW + (j + 1) * R].astype(BF16)
            if isinstance(k, int) and k == mine:
                zrs[k] = zs[b - STAY]
                zro[k] = zo[k]
            else:
                pair, dev = b - STAY, from_g(k)
                over_g(zs.at[pair], zrs.at[k], zs_s.at[0], zs_r.at[pair], dev).start()
                over_g(zo.at[k], zro.at[k], zo_s.at[0], zo_r.at[pair], dev).start()

    def give_far(_):
        @pl.loop(0, far_pairs)
        def _(i):
            give_back(STAY + turn(i))

    def end_stay(b):
        highest, total, factors = factors_of(b)
        old, new = with_new(b, highest, total)
        columns = columns_of(b, [factor * old for factor in factors] + [new])
        keep(b, blend(b, columns) + nadd[b] * columns[:, T : T + 1])

    def returned(b):
        first = (b - STAY) * BATCH
        came = pl.ds(first, BATCH - (first <= mine < first + BATCH))
        over_g(zrs.at[came], zrs.at[came], zs_s.at[0], zs_r.at[b - STAY], g).wait_recv()
        over_g(zro.at[came], zro.at[came], zo_s.at[0], zo_r.at[b - STAY], g).wait_recv()

    def end_moved(b):
        lanes = lax.broadcasted_iota(jnp.int32, (2, PW), 1)
        stats = jnp.zeros((2, PW), F32)
        first = (b - STAY) * BATCH
        for j in range(BATCH):
            stats = jnp.where((lanes // R) % BATCH == j, zrs[first + j], stats)
        blended = jnp.concatenate(
            [zro[first + j, i].astype(F32) for i in range(KVL) for j in range(BATCH)], axis=0
        )
        finish(b, stats[0:1], stats[1:2], blended)

    moved = list(range(STAY, NB))
    def stay_early(_):
        @pl.when(early)
        def _():
            arrived(0)
            end_stay(0)

    def stay_late(_):
        @pl.when(jnp.logical_not(early))
        def _():
            arrived(0)
            end_stay(0)

    plan = [(stay_early, 0), (give_far, 0), (give_back, moved[-1]), (stay_late, 0)]
    waits_long = early & (lax.rem(g, 2) == 1)

    def end_beside(_):
        returned(moved[-1])
        end_moved(moved[-1])

    def beside_soon(_):
        pl.when(jnp.logical_not(waits_long))(functools.partial(end_beside, 0))

    def beside_last(_):
        pl.when(waits_long)(functools.partial(end_beside, 0))

    plan += [(returned, b) for b in moved[1:-1]] + [(end_moved, b) for b in moved[1:-1]]
    plan += [(beside_soon, 0), (returned, moved[0])] + [(arrived, b) for b in range(1, STAY)]
    plan += [(end_moved, moved[0])] + [(end_stay, b) for b in range(1, STAY)]
    plan += [(beside_last, 0)]
    for step, p in plan:
        step(p)
    for j in range(RES_DEV):
        put(j, j)
    for l in range(MIG_DEV):
        k_of = 0
        for k in range(G):
            k_of = jnp.where(tab_s[k, 0] == RES_DEV + l, k, k_of)
        put(RES_DEV + k_of, RES_DEV + l)

    others = pl.ds(1, G - 1)
    over_g(zq.at[others], zq.at[others], zq_s.at[0], zq_r.at[0], g).wait_send()
    over_g(zrs.at[others], zrs.at[others], zs_s.at[0], zs_r.at[0], g).wait_send()
    over_g(zo.at[others], zo.at[others], zo_s.at[0], zo_r.at[0], g).wait_send()
    sent = qall.at[pl.ds(0, T - 1)]
    over_t(sent, sent, q_s.at[0], q_r.at[0], t).wait_send()
    stats, parts = rstat.at[:, rest], rbuf.at[:, rest]
    over_t(stats, stats, st_s.at[0], st_r.at[0], t).wait_send()
    over_t(parts, parts, o_s.at[0], o_r.at[0], t).wait_send()


def body(
    queries,
    new_entries,
    resident_cache,
    prefill_cache,
    resident_kept,
    kept_tokens,
    prefill_slot,
    decode_slot,
):
    G = lax.axis_size("group")
    T = lax.axis_size("tensor")
    KVL = max(1, KVH // T)
    HB = H // T
    RB = STEPS * HB
    R = RB // KVL
    LW = BATCH * R
    NB = STAY + G // BATCH
    PW = KVL * LW
    dma = pltpu.SemaphoreType.DMA
    vmem = pl.BlockSpec(memory_space=pltpu.VMEM)
    hbm = pl.BlockSpec(memory_space=pl.ANY)
    return pl.pallas_call(
        functools.partial(kernel, G, T),
        out_shape=pltpu.VMEM(queries.shape, BF16),
        in_specs=[hbm] * 8,
        out_specs=vmem,
        scratch_shapes=[
            pltpu.VMEM((3, kept_tokens.shape[0]), jnp.int32),
            pltpu.SMEM((1, resident_kept.shape[0]), jnp.int32),
            pltpu.VMEM((2 * G, 128), jnp.int32),
            pltpu.SMEM((2 * G, 128), jnp.int32),
            pltpu.VMEM(queries.shape, BF16),
            pltpu.VMEM(new_entries.shape, BF16),
            pltpu.VMEM((PER_GROUP, *resident_cache.shape[1:]), BF16),
            pltpu.VMEM((T, RES_DEV + G, RB, HD), BF16),
            pltpu.VMEM((G, RB, HD), BF16),
            pltpu.VMEM((PER_GROUP, RB, HD), F32),
            pltpu.VMEM((NB, T, KVL, LW, HD), BF16),
            pltpu.VMEM((NB, T, KVL, LW, HD), BF16),
            pltpu.VMEM((NB, T, 2, PW), F32),
            pltpu.VMEM((NB, T, 2, PW), F32),
            pltpu.VMEM((PW, 128), F32),
            pltpu.VMEM((2 * NB, -(-(T + 1) // 8) * 8, PW), F32),
            pltpu.VMEM((G, KVL, R, HD), BF16),
            pltpu.VMEM((G, KVL, R, HD), BF16),
            pltpu.VMEM((NB - STAY, 2, PW), F32),
            pltpu.VMEM((G, 2, PW), F32),
            pltpu.VMEM((NB, 2, KVL * BATCH * STEPS, HD), F32),
            pltpu.VMEM((NB, 2, PW), F32),
            pltpu.VMEM((NB, PW, HD), F32),
            pltpu.VMEM((NB * BATCH, RB, HD), F32),
            dma((5,)),
            pltpu.SemaphoreType.REGULAR((G // 2 if G & (G - 1) == 0 else G,)),
            pltpu.SemaphoreType.REGULAR((1,)),
            dma((1,)),
            dma((G,)),
            dma((1,)),
            dma((RES_DEV + G,)),
            dma((1,)),
            dma((NB,)),
            dma((1,)),
            dma((NB,)),
            dma((1,)),
            dma((NB - STAY,)),
            dma((1,)),
            dma((NB - STAY,)),
        ],
        compiler_params=pltpu.CompilerParams(collective_id=0, has_side_effects=True),
    )(
        kept_tokens[None],
        prefill_slot[None],
        decode_slot[None],
        resident_kept[None],
        queries, new_entries, resident_cache, prefill_cache)


def solution(mesh):
    in_specs = (
        P("group", None, "tensor"),
        P("group", None, None),
        P("group", "tensor", None),
        P("group", "tensor", None),
        P(),
        P(),
        P(),
        P(),
    )
    out_specs = P("group", None, "tensor")
    return jax.shard_map(body, mesh=mesh, in_specs=in_specs, out_specs=out_specs, check_vma=False)
```
